32 devices in a mesh: seq: 8 (over z, x), tensor: 4 (over y, core).
Axes of the slice: x: 2, y: 2, z: 4, core: 2. Of those that a mesh axis runs over, the one named last changes fastest.
Arguments:
- hidden_in: bfloat16 [1024, 1024], P('seq'), may hold values from -6 to 6
- seq_ids: int32 [1024], replicated, may hold values from 0 to 1, as said below
- norm_gain: float32 [1024], replicated, may hold values from 0.1 to 1.9
- w_in: bfloat16 [1024, 8, 768], P(None, 'tensor'), may hold values from -0.1875 to 0.1875
- w_ab: bfloat16 [1024, 8, 2], P(None, 'tensor'), may hold values from -0.1875 to 0.1875
- conv_w: float32 [8, 4, 512], P('tensor'), may hold values from -0.7 to 0.7
- a_log: float32 [8], P('tensor'), may hold values from -8 to 1
- dt_bias: float32 [8], P('tensor'), may hold values from -5 to 0
- out_gain: float32 [256], replicated, may hold values from 0.1 to 1.9
- w_out: bfloat16 [1024, 8, 256], P(None, 'tensor'), may hold values from -0.375 to 0.375
- ffn_gain: float32 [1024], replicated, may hold values from 0.1 to 1.9
- w_gu: bfloat16 [1024, 2, 2816], P(None, None, 'tensor'), may hold values from -0.1875 to 0.1875
- w_down: bfloat16 [1024, 2816], P(None, 'tensor'), may hold values from -0.21875 to 0.21875
- out_grad: bfloat16 [1024, 1024], P('seq'), may hold values from -6 to 6
Outputs:
- block_out: bfloat16 [1024, 1024], P('seq')
- grad_in: float32 [1024, 1024], P('seq')
- grad_norm_gain: float32 [1024], P('seq')
- grad_w_in: float32 [1024, 8, 768], P('seq', 'tensor')
- grad_w_ab: float32 [1024, 8, 2], P('seq', 'tensor')
- grad_conv_w: float32 [8, 4, 512], P('tensor')
- grad_a_log: float32 [8], P('tensor')
- grad_dt_bias: float32 [8], P('tensor')
- grad_out_gain: float32 [256], replicated
- grad_w_out: float32 [1024, 8, 256], P('seq', 'tensor')
- grad_ffn_gain: float32 [1024], P('seq')
- grad_w_gu: float32 [1024, 2, 2816], P('seq', None, 'tensor')
- grad_w_down: float32 [1024, 2816], P('seq', 'tensor')
The draws below stay inside these ranges and needn't reach their ends.
Inputs may be any that keep to these rules, and one draw needn't show every extreme that they name: `seq_ids`: non-decreasing along the tokens; the first token has 0 and the last 1.
All inputs are finite; a program needn't handle non-finite values.
Results may differ from the reference program's by a relative error of at most 0.017.
Values may be sent and summed in bfloat16 or wider, within the bound.
A program may use at most 128 MiB of HBM per device.

```python
import math
import jax
import jax.numpy as jnp
from jax import lax

D = 1024
H = 8
DK = 128
DV = 256
FF = 2816
CONV = 4
GROUP = 64
TOKENS = 1024
PROJ = 768
MIXW = 512


def draw_seq_ids(key, part):
    boundary = jax.random.randint(key, (), 1, TOKENS)
    return (jnp.arange(TOKENS) >= boundary).astype(jnp.int32)


def strengthened(entries, stream_key, source, target, parts, factor):
    owner, partner = [(jnp.arange(entries.shape[axis_at]) // (entries.shape[axis_at] // parts)).reshape([-1 if axis == axis_at else 1 for axis in range(entries.ndim)]) for axis_at in (source, target)]
    chosen = jax.random.permutation(stream_key, parts)[partner]
    strong = (owner == chosen) | (owner == (partner + parts // 2) % parts)
    return jnp.where(strong, factor * entries, entries)


def shard_levels(stream_key, dims, cuts, smallest, largest):
    level, own = 1.0, jax.random.fold_in(stream_key, 6)
    for axis_at, blocks in cuts:
        steps = jnp.exp(jax.random.uniform(jax.random.fold_in(own, axis_at), (blocks,), jnp.float32, smallest / len(cuts), largest / len(cuts)))
        level = level * jnp.repeat(steps, dims[axis_at] // blocks).reshape([-1 if axis == axis_at else 1 for axis in range(len(dims))])
    return level


def noise(own_key, extent, scale, most, cuts=(), kind=jnp.bfloat16):
    factor_of = shard_levels(own_key, extent, cuts, -0.22, 0.18) if cuts else 1.0
    entries = jax.random.normal(own_key, extent, jnp.float32) * scale * factor_of
    return jnp.minimum(jnp.maximum(entries, -most), most).astype(kind)


def heavy_noise(own_key, dims, scale, limit, shards, heavy, kind=jnp.bfloat16):
    result = scale * jax.random.normal(own_key, dims, jnp.float32)
    if shards:
        result = result * shard_levels(own_key, dims, shards, -0.22, 0.18)
    return jnp.clip(strengthened(result, jax.random.fold_in(own_key, 3), *heavy), -limit, limit).astype(kind)


def setup_inputs(seed: int = 0) -> dict:
    seeds = jax.random.split(jax.random.key(seed), 15)
    hidden_in = noise(seeds[0], (TOKENS, D), 1.0, 6.0, ((0, 8),))
    seq_ids = draw_seq_ids(jax.random.fold_in(seeds[14], 71), 0)
    norm_gain = jnp.clip(1.0 + 0.18 * jax.random.normal(seeds[2], (D,), jnp.float32), 0.1, 1.9)
    w_in = noise(seeds[3], (D, H, PROJ), D ** -0.5, 0.1875, ((1, 4),))
    w_ab = noise(seeds[4], (D, H, 2), D ** -0.5, 0.1875, ((1, 4),))
    conv_w = jnp.clip(jax.random.uniform(seeds[5], (H, CONV, MIXW), jnp.float32, -0.7, 0.7) * shard_levels(seeds[5], (H, CONV, MIXW), ((0, 4),), -0.4, 0.0), -0.7, 0.7)
    a_log = jnp.clip(-8.0 + 9.0 * jax.random.uniform(seeds[6], (H,), jnp.float32) ** shard_levels(seeds[6], (H,), ((0, 4),), -0.2, 0.2), -8.0, 1.0)
    dt_bias = jnp.clip(-5.0 + 5.0 * jax.random.uniform(seeds[7], (H,), jnp.float32) ** shard_levels(seeds[7], (H,), ((0, 4),), -0.2, 0.2), -5.0, 0.0)
    out_gain = jnp.clip(1.0 + 0.18 * jax.random.normal(seeds[8], (DV,), jnp.float32), 0.1, 1.9)
    w_out = noise(seeds[9], (D, H, DV), DV ** -0.5, 0.375, ((1, 4),))
    ffn_gain = jnp.clip(1.0 + 0.18 * jax.random.normal(seeds[10], (D,), jnp.float32), 0.1, 1.9)
    w_gu = noise(seeds[11], (D, 2, FF), D ** -0.5, 0.1875, ((2, 4),))
    w_down = noise(seeds[12], (D, FF), (FF // 4) ** -0.5, 0.21875, ((1, 4),))
    out_grad = heavy_noise(seeds[13], (TOKENS, D), 1.0, 6.0, ((0, 8),), (0, 1, 8, 2.0))
    return {"hidden_in": hidden_in, "seq_ids": seq_ids, "norm_gain": norm_gain, "w_in": w_in, "w_ab": w_ab, "conv_w": conv_w, "a_log": a_log, "dt_bias": dt_bias, "out_gain": out_gain, "w_out": w_out, "ffn_gain": ffn_gain, "w_gu": w_gu, "w_down": w_down, "out_grad": out_grad}


EPSILON = 1e-06
PRECISE = lax.Precision.HIGHEST

def rms_forward(values_in, gain):
    inv_scale = lax.rsqrt(lax.optimization_barrier(jnp.mean(values_in * values_in, axis=-1, keepdims=True)) + EPSILON)
    return (values_in * inv_scale * gain, inv_scale)

def rms_backward(values_in, inv_scale, gain, upstream):
    scaled = upstream * gain
    cubed = inv_scale * inv_scale * inv_scale
    result_grad = inv_scale * scaled - values_in * cubed * lax.optimization_barrier(jnp.mean(scaled * values_in, axis=-1, keepdims=True))
    gain_grad = lax.optimization_barrier(jnp.sum(upstream * values_in * inv_scale, axis=0))
    return (result_grad, gain_grad)

def prepare(extended, mixer_ab, conv_w, a_log, dt_bias, ids_ext):
    width = conv_w.shape[1]
    row_count = mixer_ab.shape[0]
    current = ids_ext[width - 1:]
    conv_sum = jnp.zeros((row_count,) + extended.shape[1:], jnp.float32)
    for offset in range(width):
        same_seq = (ids_ext[offset:offset + row_count] == current).astype(jnp.float32)
        conv_sum = conv_sum + extended[offset:offset + row_count] * conv_w[:, offset, :][None, :, :] * same_seq[:, None, None]
    activated = jax.nn.silu(conv_sum)
    q_raw = activated[:, :, :DK]
    k_raw = activated[:, :, DK:2 * DK]
    values = activated[:, :, 2 * DK:]
    queries = q_raw * lax.rsqrt(lax.optimization_barrier(jnp.sum(q_raw * q_raw, axis=-1, keepdims=True)) + EPSILON) * (1.0 / math.sqrt(DK))
    key_vecs = k_raw * lax.rsqrt(lax.optimization_barrier(jnp.sum(k_raw * k_raw, axis=-1, keepdims=True)) + EPSILON)
    write_rate = jax.nn.sigmoid(mixer_ab[:, :, 1])
    log_decay = -jnp.exp(a_log) * jax.nn.softplus(mixer_ab[:, :, 0] + dt_bias)
    return (queries, key_vecs, values, write_rate, log_decay)

def delta_rule(queries, key_vecs, values, write_rate, log_decay, keep_mask, state):
    total = queries.shape[0]
    blocks = total // GROUP

    def split(array_in):
        return array_in.reshape((blocks, GROUP) + array_in.shape[1:])
    positions = jnp.arange(GROUP)
    lower_incl = positions[:, None] >= positions[None, :]
    strict = positions[:, None] > positions[None, :]
    eye_block = jnp.eye(GROUP, dtype=jnp.float32)

    def advance(carried, inputs):
        q_blk, k_blk, v_blk, b_blk, g_blk, keep_blk = inputs
        cumul = jnp.cumsum(g_blk, axis=0)
        segment = jnp.cumsum(1.0 - keep_blk)
        same_seg = segment[:, None] == segment[None, :]
        spread = cumul[:, None, :] - cumul[None, :, :]
        allowed = (lower_incl & same_seg)[:, :, None]
        weights = jnp.where(allowed, jnp.exp(jnp.minimum(spread, 0.0)), 0.0)
        from_start = jnp.where((segment == 0.0)[:, None], jnp.exp(cumul), 0.0)
        key_key = jnp.einsum('ihd,jhd->ijh', k_blk, k_blk, precision=PRECISE)
        lower = jnp.where(strict[:, :, None], weights * key_key * b_blk[:, None, :], 0.0)
        prior = jnp.einsum('ihd,hde->ihe', k_blk, carried, precision=PRECISE)
        target = b_blk[:, :, None] * (v_blk - from_start[:, :, None] * prior)
        system = jnp.transpose(lower, (2, 0, 1)) + eye_block
        fresh = lax.linalg.triangular_solve(system, jnp.transpose(target, (1, 0, 2)), left_side=True, lower=True, unit_diagonal=True)
        fresh = jnp.transpose(fresh, (1, 0, 2))
        query_key = jnp.einsum('ihd,jhd->ijh', q_blk, k_blk, precision=PRECISE) * weights
        reading = from_start[:, :, None] * jnp.einsum('ihd,hde->ihe', q_blk, carried, precision=PRECISE)
        reading = reading + jnp.einsum('ijh,jhe->ihe', query_key, fresh, precision=PRECISE)
        updated = from_start[-1][:, None, None] * carried + jnp.einsum('jh,jhd,jhe->hde', weights[-1], k_blk, fresh, precision=PRECISE)
        return (updated, reading)
    final_state, readings = lax.scan(advance, state, (split(queries), split(key_vecs), split(values), split(write_rate), split(log_decay), split(keep_mask)))
    return (readings.reshape((total,) + readings.shape[2:]), final_state)

def output_gate(reading, gate_in, out_gain):
    inv_scale = lax.rsqrt(lax.optimization_barrier(jnp.mean(reading * reading, axis=-1, keepdims=True)) + EPSILON)
    return reading * inv_scale * out_gain * jax.nn.silu(gate_in)

def reference(hidden_in, seq_ids, norm_gain, w_in, w_ab, conv_w, a_log, dt_bias, out_gain, w_out, ffn_gain, w_gu, w_down, out_grad):
    width = conv_w.shape[1]
    mixer_width = conv_w.shape[2]
    ids_ext = jnp.concatenate([jnp.full((width - 1,), -1, jnp.int32), seq_ids.astype(jnp.int32)])
    keep_mask = (ids_ext[width - 1:] == ids_ext[width - 2:-1]).astype(jnp.float32)
    stream = hidden_in.astype(jnp.float32)
    normed_f, inv_one = rms_forward(stream, norm_gain)
    normed_one = normed_f.astype(jnp.bfloat16)
    normed_wide = normed_one.astype(jnp.float32)
    projected = jnp.einsum('td,dhp->thp', normed_wide, w_in.astype(jnp.float32), precision=PRECISE).astype(jnp.bfloat16)
    mixer_ab = jnp.einsum('td,dhc->thc', normed_wide, w_ab.astype(jnp.float32), precision=PRECISE)
    extended = jnp.concatenate([jnp.zeros((width - 1, H, mixer_width), jnp.float32), projected[:, :, :mixer_width].astype(jnp.float32)], axis=0)
    gate_in = projected[:, :, mixer_width:].astype(jnp.float32)

    def chain(ext_in, ab_in, conv_in, alog_in, bias_in, gate_arg, gain_arg):
        queries, key_vecs, values, write_rate, log_decay = prepare(ext_in, ab_in, conv_in, alog_in, bias_in, ids_ext)
        start_state = jnp.zeros((H, DK, DV), jnp.float32)
        reading, _ = delta_rule(queries, key_vecs, values, write_rate, log_decay, keep_mask, start_state)
        return output_gate(reading, gate_arg, gain_arg)
    gated_f, chain_back = jax.vjp(chain, extended, mixer_ab, conv_w, a_log, dt_bias, gate_in, out_gain)
    gated = gated_f.astype(jnp.bfloat16)
    mixed = jnp.einsum('the,dhe->td', gated.astype(jnp.float32), w_out.astype(jnp.float32), precision=PRECISE)
    middle = stream + mixed
    normed_two_f, inv_two = rms_forward(middle, ffn_gain)
    normed_two = normed_two_f.astype(jnp.bfloat16)
    gate_up = jnp.einsum('td,dcf->tcf', normed_two.astype(jnp.float32), w_gu.astype(jnp.float32), precision=PRECISE)
    gate_part = gate_up[:, 0]
    up_part = gate_up[:, 1]
    hidden_ffn = (jax.nn.silu(gate_part) * up_part).astype(jnp.bfloat16)
    ffn_out = jnp.dot(hidden_ffn.astype(jnp.float32), w_down.T.astype(jnp.float32), preferred_element_type=jnp.float32)
    block_out = (middle + ffn_out).astype(jnp.bfloat16)
    grad_top = out_grad.astype(jnp.float32)
    grad_w_down = jnp.dot(out_grad.T.astype(jnp.float32), hidden_ffn.astype(jnp.float32), preferred_element_type=jnp.float32)
    grad_hidden = jnp.dot(out_grad.astype(jnp.float32), w_down.astype(jnp.float32), preferred_element_type=jnp.float32)
    sigmoid_gate = jax.nn.sigmoid(gate_part)
    grad_gate_ffn = grad_hidden * up_part * sigmoid_gate * (1.0 + gate_part * (1.0 - sigmoid_gate))
    grad_up = grad_hidden * gate_part * sigmoid_gate
    grad_gate_up = jnp.stack([grad_gate_ffn, grad_up], axis=1).astype(jnp.bfloat16)
    grad_w_gu = jnp.einsum('td,tcf->dcf', normed_two.astype(jnp.float32), grad_gate_up.astype(jnp.float32), precision=PRECISE)
    grad_normed_two = jnp.einsum('tcf,dcf->td', grad_gate_up.astype(jnp.float32), w_gu.astype(jnp.float32), precision=PRECISE)
    grad_middle_norm, grad_ffn_gain = rms_backward(middle, inv_two, ffn_gain, grad_normed_two)
    grad_middle = grad_top + grad_middle_norm
    grad_middle_b = grad_middle.astype(jnp.bfloat16).astype(jnp.float32)
    grad_w_out = jnp.einsum('td,the->dhe', grad_middle_b, gated.astype(jnp.float32), precision=PRECISE)
    grad_gated = jnp.einsum('td,dhe->the', grad_middle_b, w_out.astype(jnp.float32), precision=PRECISE)
    grad_extended, grad_ab, grad_conv_w, grad_a_log, grad_dt_bias, grad_gate_in, grad_out_gain = chain_back(grad_gated)
    grad_projected = jnp.concatenate([grad_extended[width - 1:], grad_gate_in], axis=-1).astype(jnp.bfloat16).astype(jnp.float32)
    grad_ab_b = grad_ab.astype(jnp.bfloat16).astype(jnp.float32)
    grad_w_in = jnp.einsum('td,thp->dhp', normed_wide, grad_projected, precision=PRECISE)
    grad_w_ab = jnp.einsum('td,thc->dhc', normed_wide, grad_ab_b, precision=PRECISE)
    grad_normed_one = jnp.einsum('thp,dhp->td', grad_projected, w_in.astype(jnp.float32), precision=PRECISE)
    grad_normed_one = grad_normed_one + jnp.einsum('thc,dhc->td', grad_ab_b, w_ab.astype(jnp.float32), precision=PRECISE)
    grad_norm_in, grad_norm_gain = rms_backward(stream, inv_one, norm_gain, grad_normed_one)
    grad_in = grad_middle + grad_norm_in
    return (block_out, grad_in, grad_norm_gain, grad_w_in, grad_w_ab, grad_conv_w, grad_a_log, grad_dt_bias, grad_out_gain, grad_w_out, grad_ffn_gain, grad_w_gu, grad_w_down)
```

```python
import math

import jax
import jax.numpy as jnp
from jax import lax
from jax.experimental import pallas as pl
from jax.experimental.pallas import tpu as pltpu
from jax.sharding import PartitionSpec as P

DK = 128

EPSILON = 1e-06
PRECISE = lax.Precision.HIGHEST


def passed_along(block, axis, distance):
    devices = range(lax.axis_size(axis))
    route = [(i - distance, i) for i in devices if i - distance in devices]
    return lax.ppermute(block, axis, route)


def exchanged_sum(part, axis, kind):
    count = lax.axis_size(axis)
    if count & (count - 1):
        return lax.psum(part.astype(kind), axis).astype(jnp.float32)
    distance = 1
    while distance < count:
        own = part.astype(kind)
        other = lax.ppermute(own, axis, [(i, i ^ distance) for i in range(count)])
        part = own.astype(jnp.float32) + other.astype(jnp.float32)
        distance *= 2
    return part


def bf(x):
    return x.astype(jnp.bfloat16)


def wide(x):
    return x.astype(jnp.float32)


def bmm(a, b):
    return jnp.einsum("hab,hbe->hae", a, b, precision=PRECISE)


def rms_forward(values_in, gain):
    inv_scale = lax.rsqrt(jnp.mean(values_in * values_in, axis=-1, keepdims=True) + EPSILON)
    return (values_in * inv_scale * gain, inv_scale)


def rms_backward(values_in, inv_scale, gain, upstream):
    scaled = upstream * gain
    cubed = inv_scale * inv_scale * inv_scale
    result_grad = inv_scale * scaled - values_in * cubed * jnp.mean(
        scaled * values_in, axis=-1, keepdims=True
    )
    gain_grad = jnp.sum(upstream * values_in * inv_scale, axis=0)
    return (result_grad, gain_grad)


def prepare(extended, decay_in, rate_in, conv_w, a_log, dt_bias, ids_ext):
    width = conv_w.shape[1]
    row_count = decay_in.shape[1]
    current = ids_ext[width - 1 :]
    conv_sum = 0.0
    for offset in range(width):
        same_seq = (ids_ext[offset : offset + row_count] == current).astype(jnp.float32)
        conv_sum = (
            conv_sum
            + extended[:, offset : offset + row_count]
            * conv_w[:, offset, :][:, None, :]
            * same_seq[None, :, None]
        )
    activated = jax.nn.silu(conv_sum)
    q_raw = activated[:, :, :DK]
    k_raw = activated[:, :, DK : 2 * DK]
    values = activated[:, :, 2 * DK :]
    queries = (
        q_raw
        * lax.rsqrt(jnp.sum(q_raw * q_raw, axis=-1, keepdims=True) + EPSILON)
        * (1.0 / math.sqrt(DK))
    )
    key_vecs = k_raw * lax.rsqrt(jnp.sum(k_raw * k_raw, axis=-1, keepdims=True) + EPSILON)
    write_rate = jax.nn.sigmoid(rate_in)
    log_decay = -jnp.exp(a_log)[:, None] * jax.nn.softplus(decay_in + dt_bias[:, None])
    return (queries, key_vecs, values, write_rate, log_decay)


def mm(a, b, ca, cb):
    return lax.dot_general(
        a, b, (((ca,), (cb,)), ((), ())), precision=PRECISE, preferred_element_type=jnp.float32
    )


def grids(rows):
    i = lax.broadcasted_iota(jnp.int32, (rows, rows), 0)
    j = lax.broadcasted_iota(jnp.int32, (rows, rows), 1)
    return i, j


def as_col(row, eye):
    return jnp.sum(jnp.where(eye, row, 0.0), axis=1, keepdims=True)


def as_row(col, eye):
    return jnp.sum(jnp.where(eye, col, 0.0), axis=0, keepdims=True)


def block_terms(g_row, b_row, ids_row, first_row, i, j):
    eye = i == j
    g_col = as_col(g_row, eye)
    cum_col = jnp.sum(jnp.where(i >= j, g_row, 0.0), axis=1, keepdims=True)
    cum_row = jnp.sum(jnp.where(i <= j, g_col, 0.0), axis=0, keepdims=True)
    allowed = (i >= j) & (as_col(ids_row, eye) == ids_row)
    weights = jnp.where(allowed, jnp.exp(jnp.minimum(cum_col - cum_row, 0.0)), 0.0)
    from_start = as_col(first_row, eye) * jnp.exp(cum_col)
    return weights, from_start, as_col(b_row, eye)


def delta_forward_kernel(
    q_ref, k_ref, v_ref, b_ref, g_ref, ids_ref, first_ref, inv_ref, f_ref, r_ref, s_ref
):
    heads, rows, _ = q_ref.shape
    i, j = grids(rows)
    eye = i == j
    keep = []
    for h in range(heads):
        weights, from_start, b_col = block_terms(
            g_ref[h : h + 1, :], b_ref[h : h + 1, :], ids_ref[...], first_ref[...], i, j
        )
        k = k_ref[h]
        lower = jnp.where(i > j, weights * mm(k, k, 1, 1) * b_col, 0.0)
        keep.append((weights, from_start, b_col, lower))
    inverses = [jnp.where(eye, 1.0, 0.0)] * heads
    size = 1
    while size < rows:
        pair = (i // (2 * size) == j // (2 * size)) & (i // size > j // size)
        for h in range(heads):
            off = jnp.where(pair, keep[h][3], 0.0)
            if size > 1:
                off = mm(mm(inverses[h], off, 1, 0), inverses[h], 1, 0)
            inverses[h] = inverses[h] - off
        size *= 2
    for h in range(heads):
        weights, from_start, b_col, _ = keep[h]
        q, k, v = q_ref[h], k_ref[h], v_ref[h]
        target = jnp.concatenate([-(b_col * from_start) * k, b_col * v], axis=1)
        fresh = mm(inverses[h], target, 1, 0)
        query_key = mm(q, k, 1, 1) * weights
        reading = mm(query_key, fresh, 1, 0)
        last = as_col(weights[rows - 1 :, :], eye)
        state = mm(k * last, fresh, 0, 0)
        inv_ref[h] = inverses[h]
        f_ref[h] = fresh
        r_ref[h, :, :DK] = reading[:, :DK] + from_start * q
        r_ref[h, :, DK:] = reading[:, DK:]
        di, dj = grids(DK)
        own_map = state[:, :DK] + jnp.where(di == dj, from_start[rows - 1 :, :], 0.0)
        s_ref[h, :, :DK] = own_map.astype(s_ref.dtype)
        s_ref[h, :, DK:] = state[:, DK:].astype(s_ref.dtype)


def delta_backward_kernel(
    q_ref, k_ref, v_ref, b_ref, g_ref, ids_ref, first_ref, inv_ref, f_ref,
    s_ref, dr_ref, ds_ref, dq_ref, dk_ref, dv_ref, db_ref, dg_ref,
):
    heads, rows, _ = q_ref.shape
    i, j = grids(rows)
    eye = i == j
    for h in range(heads):
        weights, from_start, b_col = block_terms(
            g_ref[h : h + 1, :], b_ref[h : h + 1, :], ids_ref[...], first_ref[...], i, j
        )
        q, k, v = q_ref[h], k_ref[h], v_ref[h]
        state, d_read, d_state = s_ref[h], dr_ref[h], ds_ref[h]
        fresh = f_ref[h, :, DK:] + mm(f_ref[h, :, :DK], state, 1, 0)
        qk = mm(q, k, 1, 1)
        kk = mm(k, k, 1, 1)
        q_state = mm(q, state, 1, 0)
        k_state = mm(k, state, 1, 0)
        last = as_col(weights[rows - 1 :, :], eye)
        d_fresh = mm(qk * weights, d_read, 0, 0) + mm(k * last, d_state, 1, 0)
        d_target = mm(inv_ref[h], d_fresh, 0, 0)
        d_lower = jnp.where(i > j, -mm(d_target, fresh, 1, 1), 0.0)
        d_p = mm(d_read, fresh, 1, 1)
        d_qk = d_p * weights
        d_kk = d_lower * weights * b_col
        d_klast = mm(fresh, d_state, 1, 1)
        d_last = as_row(jnp.sum(d_klast * k, axis=1, keepdims=True), eye)
        d_w = d_p * qk + d_lower * kk * b_col + jnp.where(i == rows - 1, d_last, 0.0)
        dq_ref[h] = mm(from_start * d_read, state, 1, 1) + mm(d_qk, k, 1, 0)
        dk_ref[h] = (
            mm(-(b_col * from_start) * d_target, state, 1, 1)
            + mm(d_qk, q, 0, 0)
            + mm(d_kk, k, 1, 0)
            + mm(d_kk, k, 0, 0)
            + last * d_klast
        )
        dv_ref[h] = b_col * d_target
        d_b = jnp.sum(d_target * (v - from_start * k_state), axis=1, keepdims=True) + jnp.sum(
            d_lower * weights * kk, axis=1, keepdims=True
        )
        d_fs = jnp.sum(d_read * q_state - b_col * d_target * k_state, axis=1, keepdims=True)
        d_fs_last = jnp.sum(
            jnp.sum(d_state * state, axis=1, keepdims=True), axis=0, keepdims=True
        )
        at_end = lax.broadcasted_iota(jnp.int32, (rows, 1), 0) == rows - 1
        d_fs = d_fs + jnp.where(at_end, d_fs_last, 0.0)
        spread = d_w * weights
        d_cum = (
            jnp.sum(spread, axis=1, keepdims=True)
            - as_col(jnp.sum(spread, axis=0, keepdims=True), eye)
            + d_fs * from_start
        )
        db_ref[h : h + 1, :] = as_row(d_b, eye)
        dg_ref[h : h + 1, :] = jnp.sum(jnp.where(i >= j, d_cum, 0.0), axis=0, keepdims=True)


def f32(*shape):
    return jax.ShapeDtypeStruct(shape, jnp.float32)


def delta_forward(q, k, v, b, g, ids_row, first_row):
    heads, rows, _ = q.shape
    joined = DK + v.shape[2]
    return pl.pallas_call(
        delta_forward_kernel,
        out_shape=(
            f32(heads, rows, rows),
            f32(heads, rows, joined),
            f32(heads, rows, joined),
            jax.ShapeDtypeStruct((heads, DK, joined), jnp.bfloat16),
        ),
        name="delta_forward",
    )(q, k, v, b, g, ids_row, first_row)


def delta_backward(q, k, v, b, g, ids_row, first_row, inv, fresh, state, d_read, d_state):
    return pl.pallas_call(
        delta_backward_kernel,
        out_shape=(
            f32(*q.shape), f32(*k.shape), f32(*v.shape), f32(*b.shape), f32(*g.shape),
        ),
        name="delta_backward",
    )(q, k, v, b, g, ids_row, first_row, inv, fresh, state, d_read, d_state)


def output_gate(reading, gate_in, out_gain):
    inv_scale = lax.rsqrt(jnp.mean(reading * reading, axis=-1, keepdims=True) + EPSILON)
    return reading * inv_scale * out_gain * jax.nn.silu(gate_in)


def spans(count):
    found, span = [], 2
    while span < count - 1:
        found.append(span)
        span *= 2
    return found


def state_before(carry):
    first = wide(passed_along(carry, "seq", 1))
    second = wide(passed_along(carry, "seq", 2))
    moved = bmm(first[:, :, :DK], second)
    held_map, held_add = moved[:, :, :DK], first[:, :, DK:] + moved[:, :, DK:]
    found = [(1, carry[:, :, :DK])]
    steps = spans(lax.axis_size("seq"))
    for span in steps:
        found.append((span, bf(held_map)))
        if span == steps[-1]:
            held_add = held_add + bmm(held_map, wide(passed_along(bf(held_add), "seq", span)))
        else:
            sent = bf(jnp.concatenate([held_map, held_add], axis=-1))
            moved = bmm(held_map, wide(passed_along(sent, "seq", span)))
            held_map, held_add = moved[:, :, :DK], held_add + moved[:, :, DK:]
    maps = []
    for span, block in found:
        back = 1 if span == 1 else span + 1
        maps.append(passed_along(block, "seq", -back))
    return held_add, maps


def grad_after(carry_grad, maps):
    own = bf(carry_grad)
    flipped = [jnp.swapaxes(wide(block), 1, 2) for block in maps]
    first = wide(passed_along(own, "seq", -1))
    held = first + bmm(flipped[0], wide(passed_along(own, "seq", -2)))
    for span, here in zip(spans(lax.axis_size("seq")), flipped[1:]):
        held = held + bmm(here, wide(passed_along(bf(held), "seq", -span)))
    return held


def flipped_bit(block, distance):
    count = lax.axis_size("seq")
    return lax.ppermute(block, "seq", [(i, i ^ distance) for i in range(count)])


def owned_columns(whole, shift, group):
    rows, model = whole.shape
    share = model // lax.axis_size("seq")
    low = lax.axis_index("seq") % group
    split = whole.reshape(rows, -1, group, share)
    return lax.dynamic_index_in_dim(split, low ^ shift, 2, keepdims=False).reshape(rows, -1)


def gather_square(block, columns):
    width = block.shape[1]

    def pack(shift):
        return [owned_columns(x, shift, 4) for x in columns]

    near = flipped_bit(jnp.concatenate([block] + pack(1), axis=1), 1)
    far = flipped_bit(jnp.concatenate([block] + pack(3) + pack(2), axis=1), 2)
    extra = sum(x.shape[1] for x in pack(0))
    diagonal = flipped_bit(far[:, : width + extra], 1)
    far_own = jnp.concatenate([far[:, :width], far[:, width + extra :]], axis=1)
    own = jnp.concatenate([block] + pack(0), axis=1)
    joined = jnp.concatenate([own, near, far_own, diagonal], axis=0)
    parts, at = [joined[:, :width]], width
    for x in pack(0):
        parts.append(joined[:, at : at + x.shape[1]])
        at += x.shape[1]
    return parts


def token_product(a, b):
    return lax.dot_general(a, b, (((0,), (0,)), ((), ())), preferred_element_type=jnp.float32)


def halves_sum(partial):
    share = partial.shape[0] // 2
    high = lax.axis_index("seq") // 4
    own = lax.dynamic_slice_in_dim(partial, high * share, share, 0)
    other = lax.dynamic_slice_in_dim(partial, (1 - high) * share, share, 0)
    return own + wide(flipped_bit(bf(other), 4))


def shards(
    hidden_in,
    seq_ids,
    norm_gain,
    w_in,
    w_ab,
    conv_w,
    a_log,
    dt_bias,
    out_gain,
    w_out,
    ffn_gain,
    w_gu,
    w_down,
    out_grad,
):
    row_count, model = hidden_in.shape
    heads = w_in.shape[1]
    width = conv_w.shape[1]
    mixer_width = conv_w.shape[2]
    count = lax.axis_size("seq")
    here = lax.axis_index("seq")
    first_row = here * row_count
    padded_ids = jnp.concatenate([jnp.full((width - 1,), -1, jnp.int32), seq_ids])
    ids_ext = lax.dynamic_slice_in_dim(padded_ids, first_row, row_count + width - 1)
    own_ids = ids_ext[width - 1 :]
    ids_row = own_ids.astype(jnp.float32)[None, :]
    same_first = (own_ids == ids_ext[width - 2]).astype(jnp.float32)[None, :]
    stream = hidden_in.astype(jnp.float32)
    normed_f, inv_one = rms_forward(stream, norm_gain)
    normed_one = normed_f.astype(jnp.bfloat16)
    projected = bf(
        jnp.einsum("td,dhp->htp", normed_one, w_in, preferred_element_type=jnp.float32)
    )
    mixer_ab = jnp.einsum("td,dhc->hct", normed_one, w_ab, preferred_element_type=jnp.float32)
    mixer_cols = projected[:, :, :mixer_width]
    edge_rows = passed_along(mixer_cols[:, row_count - width + 1 :], "seq", 1)
    extended = wide(jnp.concatenate([edge_rows, mixer_cols], axis=1))
    gate_in = wide(projected[:, :, mixer_width:])

    def prepare_local(ext_in, decay_in, rate_in, conv_in, alog_in, bias_in):
        return prepare(ext_in, decay_in, rate_in, conv_in, alog_in, bias_in, ids_ext)

    prepared, prepare_back = jax.vjp(
        prepare_local, extended, mixer_ab[:, 0], mixer_ab[:, 1], conv_w, a_log, dt_bias
    )
    inverse, fresh, readings, carry = delta_forward(*prepared, ids_row, same_first)
    query_eff = readings[:, :, :DK]
    state_in, maps = state_before(carry)
    reading = readings[:, :, DK:] + bmm(query_eff, state_in)
    gated_f, gate_back = jax.vjp(output_gate, reading, gate_in, out_gain)
    gated = bf(gated_f)
    mixed_part = jnp.einsum("hte,dhe->td", gated, w_out, preferred_element_type=jnp.float32)
    mixed = exchanged_sum(mixed_part, "tensor", jnp.bfloat16)
    mixed, maps = lax.optimization_barrier((mixed, maps))
    middle = stream + mixed
    normed_two_f, inv_two = rms_forward(middle, ffn_gain)
    normed_two = bf(normed_two_f)
    gate_part = jnp.dot(normed_two, w_gu[:, 0], preferred_element_type=jnp.float32)
    up_part = jnp.dot(normed_two, w_gu[:, 1], preferred_element_type=jnp.float32)
    hidden_ffn = bf(jax.nn.silu(gate_part) * up_part)
    ffn_part = jnp.einsum("tf,df->td", hidden_ffn, w_down, preferred_element_type=jnp.float32)
    ffn_out = exchanged_sum(ffn_part, "tensor", jnp.bfloat16)
    block_out = bf(middle + ffn_out)
    grad_top = wide(out_grad)
    grad_hidden = jnp.dot(out_grad, w_down, preferred_element_type=jnp.float32)
    sigmoid_gate = jax.nn.sigmoid(gate_part)
    grad_gate_ffn = bf(
        grad_hidden * up_part * sigmoid_gate * (1.0 + gate_part * (1.0 - sigmoid_gate))
    )
    grad_up = bf(grad_hidden * gate_part * sigmoid_gate)
    normed_two_part = jnp.einsum(
        "tf,df->td", grad_gate_ffn, w_gu[:, 0], preferred_element_type=jnp.float32
    ) + jnp.einsum("tf,df->td", grad_up, w_gu[:, 1], preferred_element_type=jnp.float32)
    grad_normed_two = exchanged_sum(normed_two_part, "tensor", jnp.bfloat16)
    share = model // count
    ffn_width = w_down.shape[1]
    squared = count == 2 * 4 and share % 128 == 0
    if squared:
        ffn_block, two_cols, top_cols = gather_square(
            jnp.concatenate([grad_gate_ffn, grad_up, hidden_ffn], axis=1), [normed_two, out_grad]
        )
        ffn_share = halves_sum(
            jnp.concatenate(
                [
                    token_product(two_cols, ffn_block[:, : 2 * ffn_width]),
                    token_product(top_cols, ffn_block[:, 2 * ffn_width :]),
                ],
                axis=1,
            )
        )
    else:
        ffn_grads = jnp.concatenate(
            [
                bf(token_product(normed_two, grad_gate_ffn)),
                bf(token_product(normed_two, grad_up)),
                bf(token_product(out_grad, hidden_ffn)),
            ],
            axis=1,
        )
        ffn_share = wide(lax.psum_scatter(ffn_grads, "seq", scatter_dimension=0, tiled=True))
    share_w_gu = ffn_share[:, : 2 * ffn_width].reshape(-1, 2, ffn_width)
    share_w_down = ffn_share[:, 2 * ffn_width :]
    grad_middle_norm, grad_ffn_gain = rms_backward(middle, inv_two, ffn_gain, grad_normed_two)
    grad_middle = grad_top + grad_middle_norm
    grad_middle_b = bf(grad_middle)
    grad_gated = jnp.einsum("td,dhe->hte", grad_middle_b, w_out, preferred_element_type=jnp.float32)
    grad_reading, grad_gate_in, gain_part = gate_back(grad_gated)
    carry_grad = jnp.einsum("htd,hte->hde", query_eff, grad_reading, precision=PRECISE)
    state_grad = grad_after(carry_grad, maps)
    delta_grads = delta_backward(
        *prepared, ids_row, same_first, inverse, fresh, state_in, grad_reading, state_grad
    )
    grad_extended, grad_decay, grad_rate, grad_conv_w, grad_a_log, grad_dt_bias = prepare_back(
        tuple(delta_grads)
    )
    returned_edge = passed_along(grad_extended[:, : width - 1], "seq", -1)
    grad_mixer = jnp.concatenate(
        [
            grad_extended[:, width - 1 : row_count],
            grad_extended[:, row_count:] + returned_edge,
        ],
        axis=1,
    )
    grad_projected = bf(jnp.concatenate([grad_mixer, grad_gate_in], axis=-1))
    grad_ab_b = bf(jnp.stack([grad_decay, grad_rate], axis=1))
    if squared:
        side_block, middle_cols, one_cols = gather_square(
            jnp.concatenate([*gated, *bf(grad_gate_in)], axis=1), [grad_middle_b, normed_one]
        )
        values = w_out.shape[2] * heads
        share_side = halves_sum(
            jnp.concatenate(
                [
                    token_product(middle_cols, side_block[:, :values]),
                    token_product(one_cols, side_block[:, values:]),
                ],
                axis=1,
            )
        )
        share_w_out, share_gate = share_side[:, :values], share_side[:, values:]
        (late_block,) = gather_square(jnp.concatenate([*bf(grad_mixer)], axis=1), [])
        share_mixer = halves_sum(token_product(one_cols, late_block))
        share_w_out = share_w_out.reshape(share, heads, -1)
        share_w_in = jnp.concatenate(
            [share_mixer.reshape(share, heads, -1), share_gate.reshape(share, heads, -1)], axis=2
        )
    else:
        w_out_grad = jnp.einsum(
            "td,hte->dhe", grad_middle_b, gated, preferred_element_type=jnp.float32
        )
        w_in_grad = jnp.einsum(
            "td,htp->dhp", normed_one, grad_projected, preferred_element_type=jnp.float32
        )
        mixer_grads = jnp.concatenate(
            [bf(w_in_grad).reshape(model, -1), bf(w_out_grad).reshape(model, -1)], axis=1
        )
        mixer_share = wide(lax.psum_scatter(mixer_grads, "seq", scatter_dimension=0, tiled=True))
        in_width = heads * w_in.shape[2]
        share_w_in = mixer_share[:, :in_width].reshape(-1, heads, w_in.shape[2])
        share_w_out = mixer_share[:, in_width:].reshape(-1, heads, w_out.shape[2])
    grad_w_ab = jnp.einsum(
        "td,hct->hcd", normed_one, grad_ab_b, preferred_element_type=jnp.float32
    )
    normed_one_part = jnp.einsum(
        "htp,dhp->td", grad_projected, w_in, preferred_element_type=jnp.float32
    )
    normed_one_part = normed_one_part + jnp.einsum(
        "hct,dhc->td", grad_ab_b, w_ab, preferred_element_type=jnp.float32
    )
    grad_normed_one = exchanged_sum(normed_one_part, "tensor", jnp.bfloat16)
    gain_total = exchanged_sum(gain_part, "tensor", jnp.float32)
    grad_norm_in, grad_norm_gain = rms_backward(stream, inv_one, norm_gain, grad_normed_one)
    grad_in = grad_middle + grad_norm_in
    parts = (
        grad_conv_w, gain_total, grad_ffn_gain, grad_norm_gain, grad_w_ab, grad_a_log, grad_dt_bias,
    )
    packed = jnp.concatenate([part.reshape(-1) for part in parts])
    length = packed.shape[0]
    packed = jnp.pad(packed, (0, -length % 1024)).reshape(-1, 128)
    total = exchanged_sum(packed, "seq", jnp.float32).reshape(-1)
    pieces, at = [], 0
    for part in parts:
        pieces.append(total[at : at + part.size].reshape(part.shape))
        at += part.size
    conv_sum, gain_sum, ffn_gain_sum, norm_gain_sum, w_ab_sum, a_log_sum, dt_bias_sum = pieces
    def own(whole, dim):
        return lax.dynamic_slice_in_dim(whole, here * share, share, dim)

    return (
        block_out,
        grad_in,
        own(norm_gain_sum, 0),
        share_w_in,
        jnp.transpose(own(w_ab_sum, 2), (2, 0, 1)),
        conv_sum,
        a_log_sum,
        dt_bias_sum,
        gain_sum,
        share_w_out,
        own(ffn_gain_sum, 0),
        share_w_gu,
        share_w_down,
    )


def solution(mesh):
    return jax.shard_map(
        shards,
        mesh=mesh,
        in_specs=(
            P("seq", None),
            P(),
            P(),
            P(None, "tensor", None),
            P(None, "tensor", None),
            P("tensor", None, None),
            P("tensor"),
            P("tensor"),
            P(),
            P(None, "tensor", None),
            P(),
            P(None, None, "tensor"),
            P(None, "tensor"),
            P("seq", None),
        ),
        out_specs=(
            P("seq", None),
            P("seq", None),
            P("seq"),
            P("seq", "tensor", None),
            P("seq", "tensor", None),
            P("tensor", None, None),
            P("tensor"),
            P("tensor"),
            P(),
            P("seq", "tensor", None),
            P("seq"),
            P("seq", None, "tensor"),
            P("seq", "tensor"),
        ),
        check_vma=False,
    )
```

```python
import math

import jax
import jax.numpy as jnp
from jax import lax
from jax.experimental import pallas as pl
from jax.experimental.pallas import tpu as pltpu
from jax.sharding import PartitionSpec as P

DK = 128

EPSILON = 1e-06
PRECISE = lax.Precision.HIGHEST


def passed_along(block, axis, distance):
    devices = range(lax.axis_size(axis))
    route = [(i - distance, i) for i in devices if i - distance in devices]
    return lax.ppermute(block, axis, route)


def exchanged_sum(part, axis, kind):
    count = lax.axis_size(axis)
    if count & (count - 1):
        return lax.psum(part.astype(kind), axis).astype(jnp.float32)
    distance = 1
    while distance < count:
        own = part.astype(kind)
        other = lax.ppermute(own, axis, [(i, i ^ distance) for i in range(count)])
        part = own.astype(jnp.float32) + other.astype(jnp.float32)
        distance *= 2
    return part


def bf(x):
    return x.astype(jnp.bfloat16)


def wide(x):
    return x.astype(jnp.float32)


def bmm(a, b):
    return jnp.einsum("hab,hbe->hae", a, b, precision=PRECISE)


def rms_forward(values_in, gain):
    inv_scale = lax.rsqrt(jnp.mean(values_in * values_in, axis=-1, keepdims=True) + EPSILON)
    return (values_in * inv_scale * gain, inv_scale)


def rms_backward(values_in, inv_scale, gain, upstream):
    scaled = upstream * gain
    cubed = inv_scale * inv_scale * inv_scale
    result_grad = inv_scale * scaled - values_in * cubed * jnp.mean(
        scaled * values_in, axis=-1, keepdims=True
    )
    gain_grad = jnp.sum(upstream * values_in * inv_scale, axis=0)
    return (result_grad, gain_grad)


def prepare(extended, decay_in, rate_in, conv_w, a_log, dt_bias, ids_ext):
    width = conv_w.shape[1]
    row_count = decay_in.shape[1]
    current = ids_ext[width - 1 :]
    conv_sum = 0.0
    for offset in range(width):
        same_seq = (ids_ext[offset : offset + row_count] == current).astype(jnp.float32)
        conv_sum = (
            conv_sum
            + extended[:, offset : offset + row_count]
            * conv_w[:, offset, :][:, None, :]
            * same_seq[None, :, None]
        )
    activated = jax.nn.silu(conv_sum)
    q_raw = activated[:, :, :DK]
    k_raw = activated[:, :, DK : 2 * DK]
    values = activated[:, :, 2 * DK :]
    queries = (
        q_raw
        * lax.rsqrt(jnp.sum(q_raw * q_raw, axis=-1, keepdims=True) + EPSILON)
        * (1.0 / math.sqrt(DK))
    )
    key_vecs = k_raw * lax.rsqrt(jnp.sum(k_raw * k_raw, axis=-1, keepdims=True) + EPSILON)
    write_rate = jax.nn.sigmoid(rate_in)
    log_decay = -jnp.exp(a_log)[:, None] * jax.nn.softplus(decay_in + dt_bias[:, None])
    return (queries, key_vecs, values, write_rate, log_decay)


def mm(a, b, ca, cb):
    return lax.dot_general(
        a, b, (((ca,), (cb,)), ((), ())), precision=PRECISE, preferred_element_type=jnp.float32
    )


def grids(rows):
    i = lax.broadcasted_iota(jnp.int32, (rows, rows), 0)
    j = lax.broadcasted_iota(jnp.int32, (rows, rows), 1)
    return i, j


def as_col(row, eye):
    return jnp.sum(jnp.where(eye, row, 0.0), axis=1, keepdims=True)


def as_row(col, eye):
    return jnp.sum(jnp.where(eye, col, 0.0), axis=0, keepdims=True)


def block_terms(g_row, b_row, ids_row, first_row, i, j):
    eye = i == j
    g_col = as_col(g_row, eye)
    cum_col = jnp.sum(jnp.where(i >= j, g_row, 0.0), axis=1, keepdims=True)
    cum_row = jnp.sum(jnp.where(i <= j, g_col, 0.0), axis=0, keepdims=True)
    allowed = (i >= j) & (as_col(ids_row, eye) == ids_row)
    weights = jnp.where(allowed, jnp.exp(jnp.minimum(cum_col - cum_row, 0.0)), 0.0)
    from_start = as_col(first_row, eye) * jnp.exp(cum_col)
    return weights, from_start, as_col(b_row, eye)


def delta_forward_kernel(
    q_ref, k_ref, v_ref, b_ref, g_ref, ids_ref, first_ref, inv_ref, f_ref, r_ref, s_ref
):
    heads, rows, _ = q_ref.shape
    i, j = grids(rows)
    eye = i == j
    keep = []
    for h in range(heads):
        weights, from_start, b_col = block_terms(
            g_ref[h : h + 1, :], b_ref[h : h + 1, :], ids_ref[...], first_ref[...], i, j
        )
        k = k_ref[h]
        lower = jnp.where(i > j, weights * mm(k, k, 1, 1) * b_col, 0.0)
        keep.append((weights, from_start, b_col, lower))
    inverses = [jnp.where(eye, 1.0, 0.0)] * heads
    size = 1
    while size < rows:
        pair = (i // (2 * size) == j // (2 * size)) & (i // size > j // size)
        for h in range(heads):
            off = jnp.where(pair, keep[h][3], 0.0)
            if size > 1:
                off = mm(mm(inverses[h], off, 1, 0), inverses[h], 1, 0)
            inverses[h] = inverses[h] - off
        size *= 2
    for h in range(heads):
        weights, from_start, b_col, _ = keep[h]
        q, k, v = q_ref[h], k_ref[h], v_ref[h]
        target = jnp.concatenate([-(b_col * from_start) * k, b_col * v], axis=1)
        fresh = mm(inverses[h], target, 1, 0)
        query_key = mm(q, k, 1, 1) * weights
        reading = mm(query_key, fresh, 1, 0)
        last = as_col(weights[rows - 1 :, :], eye)
        state = mm(k * last, fresh, 0, 0)
        inv_ref[h] = inverses[h]
        f_ref[h] = fresh
        r_ref[h, :, :DK] = reading[:, :DK] + from_start * q
        r_ref[h, :, DK:] = reading[:, DK:]
        di, dj = grids(DK)
        own_map = state[:, :DK] + jnp.where(di == dj, from_start[rows - 1 :, :], 0.0)
        s_ref[h, :, :DK] = own_map.astype(s_ref.dtype)
        s_ref[h, :, DK:] = state[:, DK:].astype(s_ref.dtype)


def delta_backward_kernel(
    q_ref, k_ref, v_ref, b_ref, g_ref, ids_ref, first_ref, inv_ref, f_ref,
    s_ref, dr_ref, ds_ref, dq_ref, dk_ref, dv_ref, db_ref, dg_ref,
):
    heads, rows, _ = q_ref.shape
    i, j = grids(rows)
    eye = i == j
    for h in range(heads):
        weights, from_start, b_col = block_terms(
            g_ref[h : h + 1, :], b_ref[h : h + 1, :], ids_ref[...], first_ref[...], i, j
        )
        q, k, v = q_ref[h], k_ref[h], v_ref[h]
        state, d_read, d_state = s_ref[h], dr_ref[h], ds_ref[h]
        fresh = f_ref[h, :, DK:] + mm(f_ref[h, :, :DK], state, 1, 0)
        qk = mm(q, k, 1, 1)
        kk = mm(k, k, 1, 1)
        q_state = mm(q, state, 1, 0)
        k_state = mm(k, state, 1, 0)
        last = as_col(weights[rows - 1 :, :], eye)
        d_fresh = mm(qk * weights, d_read, 0, 0) + mm(k * last, d_state, 1, 0)
        d_target = mm(inv_ref[h], d_fresh, 0, 0)
        d_lower = jnp.where(i > j, -mm(d_target, fresh, 1, 1), 0.0)
        d_p = mm(d_read, fresh, 1, 1)
        d_qk = d_p * weights
        d_kk = d_lower * weights * b_col
        d_klast = mm(fresh, d_state, 1, 1)
        d_last = as_row(jnp.sum(d_klast * k, axis=1, keepdims=True), eye)
        d_w = d_p * qk + d_lower * kk * b_col + jnp.where(i == rows - 1, d_last, 0.0)
        dq_ref[h] = mm(from_start * d_read, state, 1, 1) + mm(d_qk, k, 1, 0)
        dk_ref[h] = (
            mm(-(b_col * from_start) * d_target, state, 1, 1)
            + mm(d_qk, q, 0, 0)
            + mm(d_kk, k, 1, 0)
            + mm(d_kk, k, 0, 0)
            + last * d_klast
        )
        dv_ref[h] = b_col * d_target
        d_b = jnp.sum(d_target * (v - from_start * k_state), axis=1, keepdims=True) + jnp.sum(
            d_lower * weights * kk, axis=1, keepdims=True
        )
        d_fs = jnp.sum(d_read * q_state - b_col * d_target * k_state, axis=1, keepdims=True)
        d_fs_last = jnp.sum(
            jnp.sum(d_state * state, axis=1, keepdims=True), axis=0, keepdims=True
        )
        at_end = lax.broadcasted_iota(jnp.int32, (rows, 1), 0) == rows - 1
        d_fs = d_fs + jnp.where(at_end, d_fs_last, 0.0)
        spread = d_w * weights
        d_cum = (
            jnp.sum(spread, axis=1, keepdims=True)
            - as_col(jnp.sum(spread, axis=0, keepdims=True), eye)
            + d_fs * from_start
        )
        db_ref[h : h + 1, :] = as_row(d_b, eye)
        dg_ref[h : h + 1, :] = jnp.sum(jnp.where(i >= j, d_cum, 0.0), axis=0, keepdims=True)


def f32(*shape):
    return jax.ShapeDtypeStruct(shape, jnp.float32)


def delta_forward(q, k, v, b, g, ids_row, first_row):
    heads, rows, _ = q.shape
    joined = DK + v.shape[2]
    return pl.pallas_call(
        delta_forward_kernel,
        out_shape=(
            f32(heads, rows, rows),
            f32(heads, rows, joined),
            f32(heads, rows, joined),
            jax.ShapeDtypeStruct((heads, DK, joined), jnp.bfloat16),
        ),
        name="delta_forward",
    )(q, k, v, b, g, ids_row, first_row)


def delta_backward(q, k, v, b, g, ids_row, first_row, inv, fresh, state, d_read, d_state):
    return pl.pallas_call(
        delta_backward_kernel,
        out_shape=(
            f32(*q.shape), f32(*k.shape), f32(*v.shape), f32(*b.shape), f32(*g.shape),
        ),
        name="delta_backward",
    )(q, k, v, b, g, ids_row, first_row, inv, fresh, state, d_read, d_state)


def output_gate(reading, gate_in, out_gain):
    inv_scale = lax.rsqrt(jnp.mean(reading * reading, axis=-1, keepdims=True) + EPSILON)
    return reading * inv_scale * out_gain * jax.nn.silu(gate_in)


def spans(count):
    found, span = [], 2
    while span < count - 1:
        found.append(span)
        span *= 2
    return found


def state_before(carry):
    first = wide(passed_along(carry, "seq", 1))
    second = wide(passed_along(carry, "seq", 2))
    moved = bmm(first[:, :, :DK], second)
    held_map, held_add = moved[:, :, :DK], first[:, :, DK:] + moved[:, :, DK:]
    found = [(1, carry[:, :, :DK])]
    steps = spans(lax.axis_size("seq"))
    for span in steps:
        found.append((span, bf(held_map)))
        if span == steps[-1]:
            held_add = held_add + bmm(held_map, wide(passed_along(bf(held_add), "seq", span)))
        else:
            sent = bf(jnp.concatenate([held_map, held_add], axis=-1))
            moved = bmm(held_map, wide(passed_along(sent, "seq", span)))
            held_map, held_add = moved[:, :, :DK], held_add + moved[:, :, DK:]
    maps = []
    for span, block in found:
        back = 1 if span == 1 else span + 1
        maps.append(passed_along(block, "seq", -back))
    return held_add, maps


def grad_after(carry_grad, maps):
    own = bf(carry_grad)
    flipped = [jnp.swapaxes(wide(block), 1, 2) for block in maps]
    first = wide(passed_along(own, "seq", -1))
    held = first + bmm(flipped[0], wide(passed_along(own, "seq", -2)))
    for span, here in zip(spans(lax.axis_size("seq")), flipped[1:]):
        held = held + bmm(here, wide(passed_along(bf(held), "seq", -span)))
    return held


def bdot(a, b, ca, cb):
    return bf(
        lax.dot_general(a, b, (((ca,), (cb,)), ((), ())), preferred_element_type=jnp.float32)
    )


def ffn_products_kernel(normed_ref, top_ref, gate_ref, up_ref, hidden_ref, out_ref):
    units = gate_ref.shape[0]
    out_ref[:units, :] = bdot(gate_ref[...], normed_ref[...], 1, 0)
    out_ref[units : 2 * units, :] = bdot(up_ref[...], normed_ref[...], 1, 0)
    out_ref[2 * units :, :] = bdot(hidden_ref[...], top_ref[...], 1, 0)


def ffn_products(normed_two, out_grad, grad_gate, grad_up, hidden, count):
    rows, model = normed_two.shape
    units, share = hidden.shape[1], model // count
    block = pl.BlockSpec((rows, share), lambda at: (0, at))
    whole = pl.BlockSpec((units, rows), lambda at: (0, 0))
    return pl.pallas_call(
        ffn_products_kernel,
        grid=(count,),
        in_specs=[block, block, whole, whole, whole],
        out_specs=pl.BlockSpec((3 * units, share), lambda at: (at, 0)),
        out_shape=jax.ShapeDtypeStruct((count * 3 * units, share), jnp.bfloat16),
        name="ffn_products",
    )(normed_two, out_grad, grad_gate.T, grad_up.T, hidden.T)


def turned(index, bit):
    return index + bit * (1 - 2 * ((index // bit) % 2))


def send(src, dst, sends, receives, at, where):
    copy = pltpu.make_async_remote_copy(
        src_ref=src,
        dst_ref=dst,
        send_sem=sends.at[at],
        recv_sem=receives.at[at],
        device_id=where,
        device_id_type=pl.DeviceIdType.MESH,
    )
    copy.start()
    return copy


def greet(axis_counts):
    barrier = pltpu.get_barrier_semaphore()
    total = 0
    for axis, count in axis_counts:
        me = lax.axis_index(axis)
        for k in range(1, count):
            pl.semaphore_signal(
                barrier, inc=1, device_id={axis: lax.rem(me + k, count)},
                device_id_type=pl.DeviceIdType.MESH,
            )
        total += count - 1
    pl.semaphore_wait(barrier, total)


def dot(a, b, ca, cb):
    return lax.dot_general(a, b, (((ca,), (cb,)), ((), ())), preferred_element_type=jnp.float32)


def tail_kernel(
    ge_ref, gate_ref, gated_ref, one_t_ref, mid_t_ref, w_ref, ab_ref, hidden_ref, gain_ref,
    middle_ref, rows_ref, pack_ref, out_gain_ref,
    in_out, out_out, grad_out, rows_out, norm_out, pack_out,
    edge_in, late_f, gd_g, gt_g, lt_g, one_g, mid_g, part_own, part_send, part_in,
    red_send, red_in, rows_in, norm_send, norm_in, pack_in, pack_own, og_in,
    sends, receives,
):
    heads, ext, mixer = ge_ref.shape
    rows = gated_ref.shape[1]
    values = gated_ref.shape[2]
    edge = ext - rows
    seqs, tensors = lax.axis_size("seq"), lax.axis_size("tensor")
    s, t = lax.axis_index("seq"), lax.axis_index("tensor")
    share = in_out.shape[0]
    low, high = s % 4, s // 4
    counter = [0]

    def push(src, dst, **where):
        at = counter[0]
        counter[0] += 1
        return send(src, dst, sends, receives, at, where)

    greet((("seq", seqs), ("tensor", tensors)))
    x_mate, z_mate = turned(s, 1), turned(s, 2)
    slot = [pl.ds(k * rows, rows) for k in range(4)]

    edge_at = counter[0]
    counter[0] += 1
    edge_copy = pltpu.make_async_remote_copy(
        src_ref=ge_ref.at[:, pl.ds(0, 8), :],
        dst_ref=edge_in,
        send_sem=sends.at[edge_at],
        recv_sem=receives.at[edge_at],
        device_id={"seq": lax.rem(s + seqs - 1, seqs)},
        device_id_type=pl.DeviceIdType.MESH,
    )
    edge_copy.start()
    og = [
        push(out_gain_ref, og_in.at[t], tensor=lax.rem(t + k, tensors)) for k in range(1, tensors)
    ]
    og_in[t] = out_gain_ref[...]

    def gather_columns(src, dst):
        copies = []
        for k, bits in ((2, (2,)), (1, (1,)), (3, (1, 2))):
            mate, want = s, low
            for bit in bits:
                mate, want = turned(mate, bit), turned(want, bit)
            for row, half in enumerate((high, 1 - high)):
                block = pl.ds(pl.multiple_of((half * 4 + want) * share, share), share)
                copies.append(
                    push(src.at[block, :], dst.at[pl.ds(row * share, share), slot[k]], seq=mate)
                )
        for row, half in enumerate((high, 1 - high)):
            block = pl.ds(pl.multiple_of((half * 4 + low) * share, share), share)
            dst[row * share : (row + 1) * share, :rows] = src[block, :]
        return copies

    far = [push(gated_ref, gd_g.at[:, slot[2], :], seq=z_mate)]
    far.append(push(gate_ref, gt_g.at[:, slot[2], :], seq=z_mate))
    near = [push(gated_ref, gd_g.at[:, slot[1], :], seq=x_mate)]
    near.append(push(gate_ref, gt_g.at[:, slot[1], :], seq=x_mate))
    for h in range(heads):
        late_f[h] = ge_ref[h, edge:, :]
        gd_g[h, :rows, :] = gated_ref[h]
        gt_g[h, :rows, :] = gate_ref[h]
    edge_copy.wait()
    has_next = jnp.where(s == seqs - 1, 0.0, 1.0)
    for h in range(heads):
        late_f[h, rows - edge :, :] += edge_in[h, :edge, :] * has_next
        lt_g[h, :rows, :] = late_f[h].astype(jnp.bfloat16)
    part = ab_ref[...]
    columns = mixer + values
    for h in range(heads):
        at = h * columns + mixer
        part = part + dot(gate_ref[h], w_ref[:, at : at + values], 1, 1)
    late_far = push(lt_g.at[:, slot[0], :], lt_g.at[:, slot[2], :], seq=z_mate)
    late_near = push(lt_g.at[:, slot[0], :], lt_g.at[:, slot[1], :], seq=x_mate)
    mid_copies = gather_columns(mid_t_ref, mid_g)
    one_copies = gather_columns(one_t_ref, one_g)
    rows_copies = []
    for k in range(1, seqs):
        to = lax.rem(s + k, seqs)
        block = pl.ds(pl.multiple_of(to * share, share), share)
        rows_copies.append(push(rows_ref.at[:, block], rows_in.at[s], seq=to))
    rows_in[s] = rows_ref[:, pl.ds(pl.multiple_of(s * share, share), share)]
    for h in range(heads):
        at = h * columns
        part = part + dot(lt_g[h, :rows, :], w_ref[:, at : at + mixer], 1, 1)

    for step in range(tensors.bit_length() - 1):
        red_send[step] = part.astype(jnp.bfloat16)
        mate = turned(t, 1 << step)
        copy = push(red_send.at[step], red_in.at[step], tensor=mate)
        if step == 0:
            for c in og:
                c.wait()
            total = og_in[0]
            for k in range(1, tensors):
                total = total + og_in[k]
            pack_own[: total.shape[0], :] = total
            pack_own[total.shape[0] :, :] = pack_ref[...]
            for c in far:
                c.wait()
            far_on = [
                push(gd_g.at[:, slot[2], :], gd_g.at[:, slot[3], :], seq=x_mate),
                push(gt_g.at[:, slot[2], :], gt_g.at[:, slot[3], :], seq=x_mate),
            ]
        else:
            late_far.wait()
            late_on = push(lt_g.at[:, slot[2], :], lt_g.at[:, slot[3], :], seq=x_mate)
            pack_copies = [
                push(pack_own, pack_in.at[s], seq=lax.rem(s + k, seqs)) for k in range(1, seqs)
            ]
            pack_in[s] = pack_own[...]
        copy.wait()
        part = red_send[step].astype(jnp.float32) + red_in[step].astype(jnp.float32)

    stream = hidden_ref[...].astype(jnp.float32)
    gain = gain_ref[...]
    inv = lax.rsqrt(jnp.mean(stream * stream, axis=-1, keepdims=True) + EPSILON)
    scaled = part * gain
    grad_out[...] = (
        middle_ref[...] + inv * scaled
        - stream * (inv * inv * inv) * jnp.mean(scaled * stream, axis=-1, keepdims=True)
    )
    gain_part = (part * stream * inv).reshape(rows // 8, 8, stream.shape[1])
    norm_send[...] = jnp.sum(gain_part, axis=0)

    exchanged = []

    def halves(copies, sources, left, block, width, at):
        for c in copies:
            c.wait()
        for h in range(heads):
            product = dot(left[...], block[h], 1, 0)
            cols = slice(at + h * width, at + (h + 1) * width)
            part_own[:, cols] = product[:share]
            part_send[:, cols] = product[share:].astype(jnp.bfloat16)
        cols = pl.ds(at, heads * width)
        exchanged.append(push(part_send.at[:, cols], part_in.at[:, cols], seq=turned(s, 4)))

    halves(mid_copies + [near[0], far_on[0]], None, mid_g, gd_g, values, 0)
    halves(one_copies + [near[1], far_on[1]], None, one_g, gt_g, values, heads * values)
    norm_copies = []
    for k in range(1, seqs):
        to = lax.rem(s + k, seqs)
        block = pl.ds(pl.multiple_of(to * share, share), share)
        norm_copies.append(push(norm_send.at[:, block], norm_in.at[s], seq=to))
    norm_in[s] = norm_send[:, pl.ds(pl.multiple_of(s * share, share), share)]
    halves([late_near, late_on], None, one_g, lt_g, mixer, 2 * heads * values)

    for c in rows_copies:
        c.wait()
    for c in pack_copies:
        c.wait()
    for ref, out in ((rows_in, rows_out), (pack_in, pack_out)):
        total = ref[0]
        for k in range(1, seqs):
            total = total + ref[k]
        out[...] = total
    for c in norm_copies:
        c.wait()
    total = norm_in[0]
    for k in range(1, seqs):
        total = total + norm_in[k]
    norm_out[...] = jnp.sum(total, axis=0, keepdims=True)

    def finish(copy, at, width, out, first):
        copy.wait()
        for h in range(heads):
            cols = slice(at + h * width, at + (h + 1) * width)
            out[:, h, first : first + width] = part_own[:, cols] + part_in[:, cols].astype(
                jnp.float32
            )

    finish(exchanged[0], 0, values, out_out, 0)
    finish(exchanged[1], heads * values, values, in_out, mixer)
    finish(exchanged[2], 2 * heads * values, mixer, in_out, 0)


def tail(ge, gate, gated, one_t, mid_t, w, ab, hidden, gain, middle, rows_small, pack, out_gain):
    heads, _, mixer = ge.shape
    _, rows, values = gated.shape
    model = hidden.shape[1]
    seqs, tensors = lax.axis_size("seq"), lax.axis_size("tensor")
    share = model // seqs
    wide_cols = heads * (mixer + 2 * values)
    joined_rows = pack.shape[0] + out_gain.shape[0]
    copies = 64
    bf16, f = jnp.bfloat16, jnp.float32
    return pl.pallas_call(
        tail_kernel,
        out_shape=(
            f32(share, heads, mixer + values),
            f32(share, heads, values),
            f32(rows, model),
            f32(rows_small.shape[0], share),
            f32(1, share),
            f32(joined_rows, pack.shape[1]),
        ),
        in_specs=[pl.BlockSpec(memory_space=pltpu.VMEM)] * 13,
        out_specs=tuple([pl.BlockSpec(memory_space=pltpu.VMEM)] * 6),
        scratch_shapes=[
            pltpu.VMEM((heads, 8, mixer), f),
            pltpu.VMEM((heads, rows, mixer), f),
            pltpu.VMEM((heads, 4 * rows, values), bf16),
            pltpu.VMEM((heads, 4 * rows, values), bf16),
            pltpu.VMEM((heads, 4 * rows, mixer), bf16),
            pltpu.VMEM((2 * share, 4 * rows), bf16),
            pltpu.VMEM((2 * share, 4 * rows), bf16),
            pltpu.VMEM((share, wide_cols), f),
            pltpu.VMEM((share, wide_cols), bf16),
            pltpu.VMEM((share, wide_cols), bf16),
            pltpu.VMEM((2, rows, model), bf16),
            pltpu.VMEM((2, rows, model), bf16),
            pltpu.VMEM((seqs, rows_small.shape[0], share), f),
            pltpu.VMEM((8, model), f),
            pltpu.VMEM((seqs, 8, share), f),
            pltpu.VMEM((seqs, joined_rows, pack.shape[1]), f),
            pltpu.VMEM((joined_rows, pack.shape[1]), f),
            pltpu.VMEM((tensors, *out_gain.shape), f),
            pltpu.SemaphoreType.DMA((copies,)),
            pltpu.SemaphoreType.DMA((copies,)),
        ],
        compiler_params=pltpu.CompilerParams(collective_id=0, has_side_effects=True),
        name="tail",
    )(ge, gate, gated, one_t, mid_t, w, ab, hidden, gain, middle, rows_small, pack, out_gain)


def shards(
    hidden_in,
    seq_ids,
    norm_gain,
    w_in,
    w_ab,
    conv_w,
    a_log,
    dt_bias,
    out_gain,
    w_out,
    ffn_gain,
    w_gu,
    w_down,
    out_grad,
):
    row_count, model = hidden_in.shape
    heads = w_in.shape[1]
    width = conv_w.shape[1]
    mixer_width = conv_w.shape[2]
    count = lax.axis_size("seq")
    here = lax.axis_index("seq")
    first_row = here * row_count
    padded_ids = jnp.concatenate([jnp.full((width - 1,), -1, jnp.int32), seq_ids])
    ids_ext = lax.dynamic_slice_in_dim(padded_ids, first_row, row_count + width - 1)
    own_ids = ids_ext[width - 1 :]
    ids_row = own_ids.astype(jnp.float32)[None, :]
    same_first = (own_ids == ids_ext[width - 2]).astype(jnp.float32)[None, :]
    stream = hidden_in.astype(jnp.float32)
    normed_f, inv_one = rms_forward(stream, norm_gain)
    normed_one = normed_f.astype(jnp.bfloat16)
    projected = bf(
        jnp.einsum("td,dhp->htp", normed_one, w_in, preferred_element_type=jnp.float32)
    )
    mixer_ab = jnp.einsum("td,dhc->hct", normed_one, w_ab, preferred_element_type=jnp.float32)
    mixer_cols = projected[:, :, :mixer_width]
    edge_rows = passed_along(mixer_cols[:, row_count - width + 1 :], "seq", 1)
    extended = wide(jnp.concatenate([edge_rows, mixer_cols], axis=1))
    gate_in = wide(projected[:, :, mixer_width:])

    def prepare_local(ext_in, decay_in, rate_in, conv_in, alog_in, bias_in):
        return prepare(ext_in, decay_in, rate_in, conv_in, alog_in, bias_in, ids_ext)

    prepared, prepare_back = jax.vjp(
        prepare_local, extended, mixer_ab[:, 0], mixer_ab[:, 1], conv_w, a_log, dt_bias
    )
    inverse, fresh, readings, carry = delta_forward(*prepared, ids_row, same_first)
    query_eff = readings[:, :, :DK]
    state_in, maps = state_before(carry)
    reading = readings[:, :, DK:] + bmm(query_eff, state_in)
    gated_f, gate_back = jax.vjp(output_gate, reading, gate_in, out_gain)
    gated = bf(gated_f)
    mixed_part = jnp.einsum("hte,dhe->td", gated, w_out, preferred_element_type=jnp.float32)
    mixed = exchanged_sum(mixed_part, "tensor", jnp.bfloat16)
    mixed, maps = lax.optimization_barrier((mixed, maps))
    middle = stream + mixed
    normed_two_f, inv_two = rms_forward(middle, ffn_gain)
    normed_two = bf(normed_two_f)
    gate_part = jnp.dot(normed_two, w_gu[:, 0], preferred_element_type=jnp.float32)
    up_part = jnp.dot(normed_two, w_gu[:, 1], preferred_element_type=jnp.float32)
    hidden_ffn = bf(jax.nn.silu(gate_part) * up_part)
    ffn_part = jnp.einsum("tf,df->td", hidden_ffn, w_down, preferred_element_type=jnp.float32)
    ffn_out = exchanged_sum(ffn_part, "tensor", jnp.bfloat16)
    block_out = bf(middle + ffn_out)
    grad_top = wide(out_grad)
    grad_hidden = jnp.dot(out_grad, w_down, preferred_element_type=jnp.float32)
    sigmoid_gate = jax.nn.sigmoid(gate_part)
    grad_gate_ffn = bf(
        grad_hidden * up_part * sigmoid_gate * (1.0 + gate_part * (1.0 - sigmoid_gate))
    )
    grad_up = bf(grad_hidden * gate_part * sigmoid_gate)
    normed_two_part = jnp.einsum(
        "tf,df->td", grad_gate_ffn, w_gu[:, 0], preferred_element_type=jnp.float32
    ) + jnp.einsum("tf,df->td", grad_up, w_gu[:, 1], preferred_element_type=jnp.float32)
    grad_normed_two = exchanged_sum(normed_two_part, "tensor", jnp.bfloat16)
    share = model // count
    ffn_width = w_down.shape[1]
    blocked = share % 128 == 0
    if blocked:
        ffn_grads = ffn_products(normed_two, out_grad, grad_gate_ffn, grad_up, hidden_ffn, count)
        ffn_share = wide(lax.psum_scatter(ffn_grads, "seq", scatter_dimension=0, tiled=True))
        share_w_gu = ffn_share[: 2 * ffn_width].reshape(2, ffn_width, share).transpose(2, 0, 1)
        share_w_down = ffn_share[2 * ffn_width :].T
    else:
        ffn_grads = jnp.concatenate(
            [
                bf(jnp.einsum("td,tf->df", normed_two, grad_gate_ffn, preferred_element_type=jnp.float32)),
                bf(jnp.einsum("td,tf->df", normed_two, grad_up, preferred_element_type=jnp.float32)),
                bf(jnp.einsum("td,tf->df", out_grad, hidden_ffn, preferred_element_type=jnp.float32)),
            ],
            axis=1,
        )
        ffn_share = wide(lax.psum_scatter(ffn_grads, "seq", scatter_dimension=0, tiled=True))
        share_w_gu = ffn_share[:, : 2 * ffn_width].reshape(-1, 2, ffn_width)
        share_w_down = ffn_share[:, 2 * ffn_width :]
    grad_middle_norm, grad_ffn_gain = rms_backward(middle, inv_two, ffn_gain, grad_normed_two)
    grad_middle = grad_top + grad_middle_norm
    grad_middle_b = bf(grad_middle)
    grad_gated = jnp.einsum("td,dhe->hte", grad_middle_b, w_out, preferred_element_type=jnp.float32)
    grad_reading, grad_gate_in, gain_part = gate_back(grad_gated)
    carry_grad = jnp.einsum("htd,hte->hde", query_eff, grad_reading, precision=PRECISE)
    state_grad = grad_after(carry_grad, maps)
    delta_grads = delta_backward(
        *prepared, ids_row, same_first, inverse, fresh, state_in, grad_reading, state_grad
    )
    grad_extended, grad_decay, grad_rate, grad_conv_w, grad_a_log, grad_dt_bias = prepare_back(
        tuple(delta_grads)
    )
    grad_ab_b = bf(jnp.stack([grad_decay, grad_rate], axis=1))
    grad_w_ab = jnp.einsum(
        "td,hct->hcd", normed_one, grad_ab_b, preferred_element_type=jnp.float32
    )
    ab_part = jnp.einsum("hct,dhc->td", grad_ab_b, w_ab, preferred_element_type=jnp.float32)
    if blocked and count == 2 * 4 and lax.axis_size("tensor") == 4:
        rows_small = jnp.concatenate(
            [grad_ffn_gain[None], grad_w_ab.reshape(2 * heads, model)], axis=0
        )
        rows_small = jnp.pad(rows_small, ((0, -rows_small.shape[0] % 8), (0, 0)))
        packed = jnp.concatenate([part.reshape(-1) for part in (grad_conv_w, grad_a_log, grad_dt_bias)])
        packed = jnp.pad(packed, (0, -packed.shape[0] % 1024)).reshape(-1, 128)
        gain_rows = jnp.pad(gain_part, (0, -gain_part.shape[0] % 1024)).reshape(-1, 128)
        share_w_in, share_w_out, grad_in, rows_sum, norm_gain_own, pack_sum = tail(
            grad_extended, bf(grad_gate_in), gated, normed_one.T, grad_middle_b.T,
            w_in.reshape(model, -1), ab_part, hidden_in, norm_gain[None], grad_middle,
            rows_small, packed, gain_rows,
        )
        flat = pack_sum.reshape(-1)
        at = gain_rows.size
        conv_end = at + grad_conv_w.size
        return (
            block_out,
            grad_in,
            norm_gain_own[0],
            share_w_in,
            jnp.transpose(rows_sum[1 : 1 + 2 * heads].reshape(heads, 2, share), (2, 0, 1)),
            flat[at:conv_end].reshape(grad_conv_w.shape),
            flat[conv_end : conv_end + heads],
            flat[conv_end + heads : conv_end + 2 * heads],
            flat[: gain_part.shape[0]],
            share_w_out,
            rows_sum[0],
            share_w_gu,
            share_w_down,
        )
    returned_edge = passed_along(grad_extended[:, : width - 1], "seq", -1)
    grad_mixer = jnp.concatenate(
        [
            grad_extended[:, width - 1 : row_count],
            grad_extended[:, row_count:] + returned_edge,
        ],
        axis=1,
    )
    grad_projected = bf(jnp.concatenate([grad_mixer, grad_gate_in], axis=-1))
    w_out_grad = jnp.einsum(
        "td,hte->dhe", grad_middle_b, gated, preferred_element_type=jnp.float32
    )
    w_in_grad = jnp.einsum(
        "td,htp->dhp", normed_one, grad_projected, preferred_element_type=jnp.float32
    )
    mixer_grads = jnp.concatenate(
        [bf(w_in_grad).reshape(model, -1), bf(w_out_grad).reshape(model, -1)], axis=1
    )
    mixer_share = wide(lax.psum_scatter(mixer_grads, "seq", scatter_dimension=0, tiled=True))
    in_width = heads * w_in.shape[2]
    share_w_in = mixer_share[:, :in_width].reshape(-1, heads, w_in.shape[2])
    share_w_out = mixer_share[:, in_width:].reshape(-1, heads, w_out.shape[2])
    normed_one_part = jnp.einsum(
        "htp,dhp->td", grad_projected, w_in, preferred_element_type=jnp.float32
    )
    normed_one_part = normed_one_part + ab_part
    grad_normed_one = exchanged_sum(normed_one_part, "tensor", jnp.bfloat16)
    gain_total = exchanged_sum(gain_part, "tensor", jnp.float32)
    grad_norm_in, grad_norm_gain = rms_backward(stream, inv_one, norm_gain, grad_normed_one)
    grad_in = grad_middle + grad_norm_in
    parts = (
        grad_conv_w, gain_total, grad_ffn_gain, grad_norm_gain, grad_w_ab, grad_a_log, grad_dt_bias,
    )
    packed = jnp.concatenate([part.reshape(-1) for part in parts])
    length = packed.shape[0]
    packed = jnp.pad(packed, (0, -length % 1024)).reshape(-1, 128)
    total = exchanged_sum(packed, "seq", jnp.float32).reshape(-1)
    pieces, at = [], 0
    for part in parts:
        pieces.append(total[at : at + part.size].reshape(part.shape))
        at += part.size
    conv_sum, gain_sum, ffn_gain_sum, norm_gain_sum, w_ab_sum, a_log_sum, dt_bias_sum = pieces
    def own(whole, dim):
        return lax.dynamic_slice_in_dim(whole, here * share, share, dim)

    return (
        block_out,
        grad_in,
        own(norm_gain_sum, 0),
        share_w_in,
        jnp.transpose(own(w_ab_sum, 2), (2, 0, 1)),
        conv_sum,
        a_log_sum,
        dt_bias_sum,
        gain_sum,
        share_w_out,
        own(ffn_gain_sum, 0),
        share_w_gu,
        share_w_down,
    )


def solution(mesh):
    return jax.shard_map(
        shards,
        mesh=mesh,
        in_specs=(
            P("seq", None),
            P(),
            P(),
            P(None, "tensor", None),
            P(None, "tensor", None),
            P("tensor", None, None),
            P("tensor"),
            P("tensor"),
            P(),
            P(None, "tensor", None),
            P(),
            P(None, None, "tensor"),
            P(None, "tensor"),
            P("seq", None),
        ),
        out_specs=(
            P("seq", None),
            P("seq", None),
            P("seq"),
            P("seq", "tensor", None),
            P("seq", "tensor", None),
            P("tensor", None, None),
            P("tensor"),
            P("tensor"),
            P(),
            P("seq", "tensor", None),
            P("seq"),
            P("seq", None, "tensor"),
            P("seq", "tensor"),
        ),
        check_vma=False,
    )
```

```python
import math

import jax
import jax.numpy as jnp
from jax import lax
from jax.experimental import pallas as pl
from jax.experimental.pallas import tpu as pltpu
from jax.sharding import PartitionSpec as P

DK = 128

EPSILON = 1e-06
PRECISE = lax.Precision.HIGHEST


def passed_along(block, axis, distance):
    devices = range(lax.axis_size(axis))
    route = [(i - distance, i) for i in devices if i - distance in devices]
    return lax.ppermute(block, axis, route)


def exchanged_sum(part, axis, kind):
    count = lax.axis_size(axis)
    if count & (count - 1):
        return lax.psum(part.astype(kind), axis).astype(jnp.float32)
    distance = 1
    while distance < count:
        own = part.astype(kind)
        other = lax.ppermute(own, axis, [(i, i ^ distance) for i in range(count)])
        part = own.astype(jnp.float32) + other.astype(jnp.float32)
        distance *= 2
    return part


def bf(x):
    return x.astype(jnp.bfloat16)


def wide(x):
    return x.astype(jnp.float32)


def bmm(a, b):
    return jnp.einsum("hab,hbe->hae", a, b, precision=PRECISE)


def rms_forward(values_in, gain):
    inv_scale = lax.rsqrt(jnp.mean(values_in * values_in, axis=-1, keepdims=True) + EPSILON)
    return (values_in * inv_scale * gain, inv_scale)


def rms_backward(values_in, inv_scale, gain, upstream):
    scaled = upstream * gain
    cubed = inv_scale * inv_scale * inv_scale
    result_grad = inv_scale * scaled - values_in * cubed * jnp.mean(
        scaled * values_in, axis=-1, keepdims=True
    )
    gain_grad = jnp.sum(upstream * values_in * inv_scale, axis=0)
    return (result_grad, gain_grad)


def prepare(extended, decay_in, rate_in, conv_w, a_log, dt_bias, ids_ext):
    width = conv_w.shape[1]
    row_count = decay_in.shape[1]
    current = ids_ext[width - 1 :]
    conv_sum = 0.0
    for offset in range(width):
        same_seq = (ids_ext[offset : offset + row_count] == current).astype(jnp.float32)
        conv_sum = (
            conv_sum
            + extended[:, offset : offset + row_count]
            * conv_w[:, offset, :][:, None, :]
            * same_seq[None, :, None]
        )
    activated = jax.nn.silu(conv_sum)
    q_raw = activated[:, :, :DK]
    k_raw = activated[:, :, DK : 2 * DK]
    values = activated[:, :, 2 * DK :]
    queries = (
        q_raw
        * lax.rsqrt(jnp.sum(q_raw * q_raw, axis=-1, keepdims=True) + EPSILON)
        * (1.0 / math.sqrt(DK))
    )
    key_vecs = k_raw * lax.rsqrt(jnp.sum(k_raw * k_raw, axis=-1, keepdims=True) + EPSILON)
    write_rate = jax.nn.sigmoid(rate_in)
    log_decay = -jnp.exp(a_log)[:, None] * jax.nn.softplus(decay_in + dt_bias[:, None])
    return (queries, key_vecs, values, write_rate, log_decay)


def mm(a, b, ca, cb):
    return lax.dot_general(
        a, b, (((ca,), (cb,)), ((), ())), precision=PRECISE, preferred_element_type=jnp.float32
    )


def grids(rows):
    i = lax.broadcasted_iota(jnp.int32, (rows, rows), 0)
    j = lax.broadcasted_iota(jnp.int32, (rows, rows), 1)
    return i, j


def as_col(row, eye):
    return jnp.sum(jnp.where(eye, row, 0.0), axis=1, keepdims=True)


def as_row(col, eye):
    return jnp.sum(jnp.where(eye, col, 0.0), axis=0, keepdims=True)


def block_terms(g_row, b_row, ids_row, first_row, i, j):
    eye = i == j
    g_col = as_col(g_row, eye)
    cum_col = jnp.sum(jnp.where(i >= j, g_row, 0.0), axis=1, keepdims=True)
    cum_row = jnp.sum(jnp.where(i <= j, g_col, 0.0), axis=0, keepdims=True)
    allowed = (i >= j) & (as_col(ids_row, eye) == ids_row)
    weights = jnp.where(allowed, jnp.exp(jnp.minimum(cum_col - cum_row, 0.0)), 0.0)
    from_start = as_col(first_row, eye) * jnp.exp(cum_col)
    return weights, from_start, as_col(b_row, eye)


def delta_forward_kernel(
    q_ref, k_ref, v_ref, b_ref, g_ref, ids_ref, first_ref, inv_ref, f_ref, r_ref, s_ref
):
    heads, rows, _ = q_ref.shape
    i, j = grids(rows)
    eye = i == j
    keep = []
    for h in range(heads):
        weights, from_start, b_col = block_terms(
            g_ref[h : h + 1, :], b_ref[h : h + 1, :], ids_ref[...], first_ref[...], i, j
        )
        k = k_ref[h]
        lower = jnp.where(i > j, weights * mm(k, k, 1, 1) * b_col, 0.0)
        keep.append((weights, from_start, b_col, lower))
    inverses = [jnp.where(eye, 1.0, 0.0)] * heads
    size = 1
    while size < rows:
        pair = (i // (2 * size) == j // (2 * size)) & (i // size > j // size)
        for h in range(heads):
            off = jnp.where(pair, keep[h][3], 0.0)
            if size > 1:
                off = mm(mm(inverses[h], off, 1, 0), inverses[h], 1, 0)
            inverses[h] = inverses[h] - off
        size *= 2
    for h in range(heads):
        weights, from_start, b_col, _ = keep[h]
        q, k, v = q_ref[h], k_ref[h], v_ref[h]
        target = jnp.concatenate([-(b_col * from_start) * k, b_col * v], axis=1)
        fresh = mm(inverses[h], target, 1, 0)
        query_key = mm(q, k, 1, 1) * weights
        reading = mm(query_key, fresh, 1, 0)
        last = as_col(weights[rows - 1 :, :], eye)
        state = mm(k * last, fresh, 0, 0)
        inv_ref[h] = inverses[h]
        f_ref[h] = fresh
        r_ref[h, :, :DK] = reading[:, :DK] + from_start * q
        r_ref[h, :, DK:] = reading[:, DK:]
        di, dj = grids(DK)
        own_map = state[:, :DK] + jnp.where(di == dj, from_start[rows - 1 :, :], 0.0)
        s_ref[h, :, :DK] = own_map.astype(s_ref.dtype)
        s_ref[h, :, DK:] = state[:, DK:].astype(s_ref.dtype)


def delta_backward_kernel(
    q_ref, k_ref, v_ref, b_ref, g_ref, ids_ref, first_ref, inv_ref, f_ref,
    s_ref, dr_ref, ds_ref, dq_ref, dk_ref, dv_ref, db_ref, dg_ref,
):
    heads, rows, _ = q_ref.shape
    i, j = grids(rows)
    eye = i == j
    for h in range(heads):
        weights, from_start, b_col = block_terms(
            g_ref[h : h + 1, :], b_ref[h : h + 1, :], ids_ref[...], first_ref[...], i, j
        )
        q, k, v = q_ref[h], k_ref[h], v_ref[h]
        state, d_read, d_state = s_ref[h], dr_ref[h], ds_ref[h]
        fresh = f_ref[h, :, DK:] + mm(f_ref[h, :, :DK], state, 1, 0)
        qk = mm(q, k, 1, 1)
        kk = mm(k, k, 1, 1)
        q_state = mm(q, state, 1, 0)
        k_state = mm(k, state, 1, 0)
        last = as_col(weights[rows - 1 :, :], eye)
        d_fresh = mm(qk * weights, d_read, 0, 0) + mm(k * last, d_state, 1, 0)
        d_target = mm(inv_ref[h], d_fresh, 0, 0)
        d_lower = jnp.where(i > j, -mm(d_target, fresh, 1, 1), 0.0)
        d_p = mm(d_read, fresh, 1, 1)
        d_qk = d_p * weights
        d_kk = d_lower * weights * b_col
        d_klast = mm(fresh, d_state, 1, 1)
        d_last = as_row(jnp.sum(d_klast * k, axis=1, keepdims=True), eye)
        d_w = d_p * qk + d_lower * kk * b_col + jnp.where(i == rows - 1, d_last, 0.0)
        dq_ref[h] = mm(from_start * d_read, state, 1, 1) + mm(d_qk, k, 1, 0)
        dk_ref[h] = (
            mm(-(b_col * from_start) * d_target, state, 1, 1)
            + mm(d_qk, q, 0, 0)
            + mm(d_kk, k, 1, 0)
            + mm(d_kk, k, 0, 0)
            + last * d_klast
        )
        dv_ref[h] = b_col * d_target
        d_b = jnp.sum(d_target * (v - from_start * k_state), axis=1, keepdims=True) + jnp.sum(
            d_lower * weights * kk, axis=1, keepdims=True
        )
        d_fs = jnp.sum(d_read * q_state - b_col * d_target * k_state, axis=1, keepdims=True)
        d_fs_last = jnp.sum(
            jnp.sum(d_state * state, axis=1, keepdims=True), axis=0, keepdims=True
        )
        at_end = lax.broadcasted_iota(jnp.int32, (rows, 1), 0) == rows - 1
        d_fs = d_fs + jnp.where(at_end, d_fs_last, 0.0)
        spread = d_w * weights
        d_cum = (
            jnp.sum(spread, axis=1, keepdims=True)
            - as_col(jnp.sum(spread, axis=0, keepdims=True), eye)
            + d_fs * from_start
        )
        db_ref[h : h + 1, :] = as_row(d_b, eye)
        dg_ref[h : h + 1, :] = jnp.sum(jnp.where(i >= j, d_cum, 0.0), axis=0, keepdims=True)


def f32(*shape):
    return jax.ShapeDtypeStruct(shape, jnp.float32)


def delta_forward(q, k, v, b, g, ids_row, first_row):
    heads, rows, _ = q.shape
    joined = DK + v.shape[2]
    return pl.pallas_call(
        delta_forward_kernel,
        out_shape=(
            f32(heads, rows, rows),
            f32(heads, rows, joined),
            f32(heads, rows, joined),
            jax.ShapeDtypeStruct((heads, DK, joined), jnp.bfloat16),
        ),
        name="delta_forward",
    )(q, k, v, b, g, ids_row, first_row)


def delta_backward(q, k, v, b, g, ids_row, first_row, inv, fresh, state, d_read, d_state):
    return pl.pallas_call(
        delta_backward_kernel,
        out_shape=(
            f32(*q.shape), f32(*k.shape), f32(*v.shape), f32(*b.shape), f32(*g.shape),
        ),
        name="delta_backward",
    )(q, k, v, b, g, ids_row, first_row, inv, fresh, state, d_read, d_state)


def output_gate(reading, gate_in, out_gain):
    inv_scale = lax.rsqrt(jnp.mean(reading * reading, axis=-1, keepdims=True) + EPSILON)
    return reading * inv_scale * out_gain * jax.nn.silu(gate_in)


def spans(count):
    found, span = [], 2
    while span < count - 1:
        found.append(span)
        span *= 2
    return found


def state_before(carry):
    first = wide(passed_along(carry, "seq", 1))
    second = wide(passed_along(carry, "seq", 2))
    moved = bmm(first[:, :, :DK], second)
    held_map, held_add = moved[:, :, :DK], first[:, :, DK:] + moved[:, :, DK:]
    found = [(1, carry[:, :, :DK])]
    steps = spans(lax.axis_size("seq"))
    for span in steps:
        found.append((span, bf(held_map)))
        if span == steps[-1]:
            held_add = held_add + bmm(held_map, wide(passed_along(bf(held_add), "seq", span)))
        else:
            sent = bf(jnp.concatenate([held_map, held_add], axis=-1))
            moved = bmm(held_map, wide(passed_along(sent, "seq", span)))
            held_map, held_add = moved[:, :, :DK], held_add + moved[:, :, DK:]
    maps = []
    for span, block in found:
        back = 1 if span == 1 else span + 1
        maps.append(passed_along(block, "seq", -back))
    return held_add, maps


def grad_after(carry_grad, maps):
    own = bf(carry_grad)
    flipped = [jnp.swapaxes(wide(block), 1, 2) for block in maps]
    first = wide(passed_along(own, "seq", -1))
    held = first + bmm(flipped[0], wide(passed_along(own, "seq", -2)))
    for span, here in zip(spans(lax.axis_size("seq")), flipped[1:]):
        held = held + bmm(here, wide(passed_along(bf(held), "seq", -span)))
    return held


def bdot(a, b, ca, cb):
    return bf(
        lax.dot_general(a, b, (((ca,), (cb,)), ((), ())), preferred_element_type=jnp.float32)
    )


def ffn_products_kernel(normed_ref, top_ref, gate_ref, up_ref, hidden_ref, out_ref):
    units = gate_ref.shape[0]
    out_ref[:units, :] = bdot(gate_ref[...], normed_ref[...], 1, 0)
    out_ref[units : 2 * units, :] = bdot(up_ref[...], normed_ref[...], 1, 0)
    out_ref[2 * units :, :] = bdot(hidden_ref[...], top_ref[...], 1, 0)


def ffn_products(normed_two, out_grad, grad_gate, grad_up, hidden, count):
    rows, model = normed_two.shape
    units, share = hidden.shape[1], model // count
    block = pl.BlockSpec((rows, share), lambda at: (0, at))
    whole = pl.BlockSpec((units, rows), lambda at: (0, 0))
    return pl.pallas_call(
        ffn_products_kernel,
        grid=(count,),
        in_specs=[block, block, whole, whole, whole],
        out_specs=pl.BlockSpec((3 * units, share), lambda at: (at, 0)),
        out_shape=jax.ShapeDtypeStruct((count * 3 * units, share), jnp.bfloat16),
        name="ffn_products",
    )(normed_two, out_grad, grad_gate.T, grad_up.T, hidden.T)


def turned(index, bit):
    return index + bit * (1 - 2 * ((index // bit) % 2))


def send(src, dst, sends, receives, at, where):
    copy = pltpu.make_async_remote_copy(
        src_ref=src,
        dst_ref=dst,
        send_sem=sends.at[at],
        recv_sem=receives.at[at],
        device_id=where,
        device_id_type=pl.DeviceIdType.MESH,
    )
    copy.start()
    return copy


def greet(axis_counts):
    barrier = pltpu.get_barrier_semaphore()
    total = 0
    for axis, count in axis_counts:
        me = lax.axis_index(axis)
        for k in range(1, count):
            pl.semaphore_signal(
                barrier, inc=1, device_id={axis: lax.rem(me + k, count)},
                device_id_type=pl.DeviceIdType.MESH,
            )
        total += count - 1
    pl.semaphore_wait(barrier, total)


def dot(a, b, ca, cb):
    return lax.dot_general(a, b, (((ca,), (cb,)), ((), ())), preferred_element_type=jnp.float32)


def greet_line():
    seqs = lax.axis_size("seq")
    s = lax.axis_index("seq")
    z, last = s // 2, seqs // 2 - 1
    barrier = pltpu.get_barrier_semaphore()

    def hail(where):
        pl.semaphore_signal(
            barrier, inc=1, device_id={"seq": where}, device_id_type=pl.DeviceIdType.MESH
        )

    hail(turned(s, 1))

    @pl.when(z > 0)
    def _():
        hail(s - 2)

    @pl.when(z < last)
    def _():
        hail(s + 2)

    pl.semaphore_wait(barrier, 1 + (z + last) // (last + 1) + (2 * last - z) // (last + 1))


def remote(src, dst, sends, receives, at, where):
    return pltpu.make_async_remote_copy(
        src_ref=src,
        dst_ref=dst,
        send_sem=sends.at[at],
        recv_sem=receives.at[at],
        device_id={"seq": where},
        device_id_type=pl.DeviceIdType.MESH,
    )


def mixer_forward_kernel(
    q_ref, k_ref, v_ref, b_ref, g_ref, ids_ref, first_ref,
    inv_ref, f_ref, eff_ref, r_ref, state_ref, map_ref,
    carry, mate, onward, arrived, sends, receives,
):
    heads, rows, _ = q_ref.shape
    s = lax.axis_index("seq")
    z, last = s // 2, lax.axis_size("seq") // 2 - 1
    lane = s % 2
    greet_line()
    i, j = grids(rows)
    eye = i == j
    keep = []
    for h in range(heads):
        weights, from_start, b_col = block_terms(
            g_ref[h : h + 1, :], b_ref[h : h + 1, :], ids_ref[...], first_ref[...], i, j
        )
        k = k_ref[h]
        lower = jnp.where(i > j, weights * mm(k, k, 1, 1) * b_col, 0.0)
        keep.append((weights, from_start, b_col, lower))
    inverses = [jnp.where(eye, 1.0, 0.0)] * heads
    size = 1
    while size < rows:
        pair = (i // (2 * size) == j // (2 * size)) & (i // size > j // size)
        for h in range(heads):
            off = jnp.where(pair, keep[h][3], 0.0)
            if size > 1:
                off = mm(mm(inverses[h], off, 1, 0), inverses[h], 1, 0)
            inverses[h] = inverses[h] - off
        size *= 2
    freshes, swaps = [], []
    di, dj = grids(DK)
    for h in range(heads):
        weights, from_start, b_col, _ = keep[h]
        k, v = k_ref[h], v_ref[h]
        target = jnp.concatenate([-(b_col * from_start) * k, b_col * v], axis=1)
        fresh = mm(inverses[h], target, 1, 0)
        end = as_col(weights[rows - 1 :, :], eye)
        state = mm(k * end, fresh, 0, 0)
        own_map = state[:, :DK] + jnp.where(di == dj, from_start[rows - 1 :, :], 0.0)
        carry[h, :, :DK] = bf(own_map)
        carry[h, :, DK:] = bf(state[:, DK:])
        freshes.append(fresh)
        swap = remote(carry.at[h], mate.at[h], sends, receives, h, turned(s, 1))
        swap.start()
        swaps.append(swap)

    @pl.when(z == 0)
    def _():
        arrived[...] = jnp.zeros_like(arrived)

    for h in range(heads):
        weights, from_start, _, _ = keep[h]
        q = q_ref[h]
        reading = mm(mm(q, k_ref[h], 1, 1) * weights, freshes[h], 1, 0)
        inv_ref[h] = inverses[h]
        f_ref[h] = freshes[h]
        eff_ref[h] = reading[:, :DK] + from_start * q
        r_ref[h] = reading[:, DK:]
    adds = []
    for h in range(heads):
        swaps[h].wait()
        own, other = wide(carry[h]), wide(mate[h])
        one = jnp.where(lane == 0, own, other)
        two = jnp.where(lane == 0, other, own)
        joined = mm(two[:, :DK], one, 1, 0)
        map_ref[0, h] = one[:, :DK]
        map_ref[1, h] = two[:, :DK]
        map_ref[2, h] = joined[:, :DK]
        adds.append((one[:, DK:], joined[:, DK:] + two[:, DK:]))
    hops = [
        remote(onward.at[h], arrived.at[h], sends, receives, heads + h, lax.rem(s + 2, 2 * last + 2))
        for h in range(heads)
    ]
    for h in range(heads):

        @pl.when(z > 0)
        def _():
            hops[h].wait_recv()

        held = wide(arrived[h])

        @pl.when(z < last)
        def _():
            onward[h] = bf(adds[h][1] + mm(map_ref[2, h], held, 1, 0))
            hops[h].start()

        state_ref[h] = jnp.where(lane == 0, held, adds[h][0] + mm(map_ref[0, h], held, 1, 0))
    for h in range(heads):
        r_ref[h] += mm(eff_ref[h], state_ref[h], 1, 0)

        @pl.when(z < last)
        def _():
            hops[h].wait_send()


def mixer_forward(q, k, v, b, g, ids_row, first_row):
    heads, rows, _ = q.shape
    values = v.shape[2]
    bf16 = jnp.bfloat16
    return pl.pallas_call(
        mixer_forward_kernel,
        out_shape=(
            f32(heads, rows, rows),
            f32(heads, rows, DK + values),
            f32(heads, rows, DK),
            f32(heads, rows, values),
            f32(heads, DK, values),
            f32(3, heads, DK, DK),
        ),
        scratch_shapes=[
            pltpu.VMEM((heads, DK, DK + values), bf16),
            pltpu.VMEM((heads, DK, DK + values), bf16),
            pltpu.VMEM((heads, DK, values), bf16),
            pltpu.VMEM((heads, DK, values), bf16),
            pltpu.SemaphoreType.DMA((2 * heads,)),
            pltpu.SemaphoreType.DMA((2 * heads,)),
        ],
        compiler_params=pltpu.CompilerParams(collective_id=1, has_side_effects=True),
        name="mixer_forward",
    )(q, k, v, b, g, ids_row, first_row)


def mixer_backward_kernel(
    q_ref, k_ref, v_ref, b_ref, g_ref, ids_ref, first_ref, inv_ref, f_ref, eff_ref,
    s_ref, map_ref, dr_ref, dq_ref, dk_ref, dv_ref, db_ref, dg_ref,
    carry, mate, onward, arrived, sends, receives,
):
    heads, rows, _ = q_ref.shape
    s = lax.axis_index("seq")
    z, last = s // 2, lax.axis_size("seq") // 2 - 1
    lane = s % 2
    greet_line()
    swaps = []
    for h in range(heads):
        carry[h] = bf(mm(eff_ref[h], dr_ref[h], 0, 0))
        swap = remote(carry.at[h], mate.at[h], sends, receives, h, turned(s, 1))
        swap.start()
        swaps.append(swap)

    @pl.when(z == last)
    def _():
        arrived[...] = jnp.zeros_like(arrived)

    i, j = grids(rows)
    eye = i == j
    early = []
    for h in range(heads):
        weights, from_start, b_col = block_terms(
            g_ref[h : h + 1, :], b_ref[h : h + 1, :], ids_ref[...], first_ref[...], i, j
        )
        q, k = q_ref[h], k_ref[h]
        state, d_read = s_ref[h], dr_ref[h]
        fresh = f_ref[h, :, DK:] + mm(f_ref[h, :, :DK], state, 1, 0)
        qk = mm(q, k, 1, 1)
        kk = mm(k, k, 1, 1)
        d_p = mm(d_read, fresh, 1, 1)
        d_fresh = mm(qk * weights, d_read, 0, 0)
        early.append((weights, from_start, b_col, fresh, qk, kk, d_p, d_fresh))
    firsts, joints = [], []
    for h in range(heads):
        swaps[h].wait()
        own, other = wide(carry[h]), wide(mate[h])
        one = jnp.where(lane == 0, own, other)
        two = jnp.where(lane == 0, other, own)
        firsts.append(two)
        joints.append(one + mm(map_ref[0, h], two, 0, 0))
    hops = [
        remote(
            onward.at[h], arrived.at[h], sends, receives, heads + h,
            lax.rem(s + 2 * last, 2 * last + 2),
        )
        for h in range(heads)
    ]
    for h in range(heads):

        @pl.when(z < last)
        def _():
            hops[h].wait_recv()

        held = wide(arrived[h])

        @pl.when(z > 0)
        def _():
            onward[h] = bf(joints[h] + mm(map_ref[2, h], held, 0, 0))
            hops[h].start()

        firsts[h] = jnp.where(lane == 1, held, firsts[h] + mm(map_ref[1, h], held, 0, 0))
    for h in range(heads):
        weights, from_start, b_col, fresh, qk, kk, d_p, d_fresh = early[h]
        q, k, v = q_ref[h], k_ref[h], v_ref[h]
        state, d_read, d_state = s_ref[h], dr_ref[h], firsts[h]
        q_state = mm(q, state, 1, 0)
        k_state = mm(k, state, 1, 0)
        end = as_col(weights[rows - 1 :, :], eye)
        d_fresh = d_fresh + mm(k * end, d_state, 1, 0)
        d_target = mm(inv_ref[h], d_fresh, 0, 0)
        d_lower = jnp.where(i > j, -mm(d_target, fresh, 1, 1), 0.0)
        d_qk = d_p * weights
        d_kk = d_lower * weights * b_col
        d_klast = mm(fresh, d_state, 1, 1)
        d_last = as_row(jnp.sum(d_klast * k, axis=1, keepdims=True), eye)
        d_w = d_p * qk + d_lower * kk * b_col + jnp.where(i == rows - 1, d_last, 0.0)
        dq_ref[h] = mm(from_start * d_read, state, 1, 1) + mm(d_qk, k, 1, 0)
        dk_ref[h] = (
            mm(-(b_col * from_start) * d_target, state, 1, 1)
            + mm(d_qk, q, 0, 0)
            + mm(d_kk, k, 1, 0)
            + mm(d_kk, k, 0, 0)
            + end * d_klast
        )
        dv_ref[h] = b_col * d_target
        d_b = jnp.sum(d_target * (v - from_start * k_state), axis=1, keepdims=True) + jnp.sum(
            d_lower * weights * kk, axis=1, keepdims=True
        )
        d_fs = jnp.sum(d_read * q_state - b_col * d_target * k_state, axis=1, keepdims=True)
        d_fs_last = jnp.sum(
            jnp.sum(d_state * state, axis=1, keepdims=True), axis=0, keepdims=True
        )
        at_end = lax.broadcasted_iota(jnp.int32, (rows, 1), 0) == rows - 1
        d_fs = d_fs + jnp.where(at_end, d_fs_last, 0.0)
        spread = d_w * weights
        d_cum = (
            jnp.sum(spread, axis=1, keepdims=True)
            - as_col(jnp.sum(spread, axis=0, keepdims=True), eye)
            + d_fs * from_start
        )
        db_ref[h : h + 1, :] = as_row(d_b, eye)
        dg_ref[h : h + 1, :] = jnp.sum(jnp.where(i >= j, d_cum, 0.0), axis=0, keepdims=True)

        @pl.when(z > 0)
        def _():
            hops[h].wait_send()


def mixer_backward(q, k, v, b, g, ids_row, first_row, inv, fresh, eff, state, maps, d_read):
    heads, _, values = v.shape
    bf16 = jnp.bfloat16
    return pl.pallas_call(
        mixer_backward_kernel,
        out_shape=(
            f32(*q.shape), f32(*k.shape), f32(*v.shape), f32(*b.shape), f32(*g.shape),
        ),
        scratch_shapes=[pltpu.VMEM((heads, DK, values), bf16)] * 4
        + [pltpu.SemaphoreType.DMA((2 * heads,))] * 2,
        compiler_params=pltpu.CompilerParams(collective_id=2, has_side_effects=True),
        name="mixer_backward",
    )(q, k, v, b, g, ids_row, first_row, inv, fresh, eff, state, maps, d_read)


def tail_kernel(
    ge_ref, gate_ref, gated_ref, one_t_ref, mid_t_ref, w_ref, ab_ref, hidden_ref, gain_ref,
    middle_ref, rows_ref, pack_ref, out_gain_ref,
    in_out, out_out, grad_out, rows_out, norm_out, pack_out,
    edge_in, late_f, gd_g, gt_g, lt_g, one_g, mid_g, part_own, part_send, part_in,
    red_send, red_in, rows_in, norm_send, norm_in, pack_in, pack_own, og_in,
    sends, receives,
):
    heads, ext, mixer = ge_ref.shape
    rows = gated_ref.shape[1]
    values = gated_ref.shape[2]
    edge = ext - rows
    seqs, tensors = lax.axis_size("seq"), lax.axis_size("tensor")
    s, t = lax.axis_index("seq"), lax.axis_index("tensor")
    share = in_out.shape[0]
    low, high = s % 4, s // 4
    counter = [0]

    def push(src, dst, **where):
        at = counter[0]
        counter[0] += 1
        return send(src, dst, sends, receives, at, where)

    greet((("seq", seqs), ("tensor", tensors)))
    x_mate, z_mate = turned(s, 1), turned(s, 2)
    slot = [pl.ds(k * rows, rows) for k in range(4)]

    edge_at = counter[0]
    counter[0] += 1
    edge_copy = pltpu.make_async_remote_copy(
        src_ref=ge_ref.at[:, pl.ds(0, 8), :],
        dst_ref=edge_in,
        send_sem=sends.at[edge_at],
        recv_sem=receives.at[edge_at],
        device_id={"seq": lax.rem(s + seqs - 1, seqs)},
        device_id_type=pl.DeviceIdType.MESH,
    )
    edge_copy.start()
    og = [
        push(out_gain_ref, og_in.at[t], tensor=lax.rem(t + k, tensors)) for k in range(1, tensors)
    ]
    og_in[t] = out_gain_ref[...]

    def gather_columns(src, dst):
        copies = []
        for k, bits in ((2, (2,)), (1, (1,)), (3, (1, 2))):
            mate, want = s, low
            for bit in bits:
                mate, want = turned(mate, bit), turned(want, bit)
            for row, half in enumerate((high, 1 - high)):
                block = pl.ds(pl.multiple_of((half * 4 + want) * share, share), share)
                copies.append(
                    push(src.at[block, :], dst.at[pl.ds(row * share, share), slot[k]], seq=mate)
                )
        for row, half in enumerate((high, 1 - high)):
            block = pl.ds(pl.multiple_of((half * 4 + low) * share, share), share)
            dst[row * share : (row + 1) * share, :rows] = src[block, :]
        return copies

    far = [push(gated_ref, gd_g.at[:, slot[2], :], seq=z_mate)]
    far.append(push(gate_ref, gt_g.at[:, slot[2], :], seq=z_mate))
    near = [push(gated_ref, gd_g.at[:, slot[1], :], seq=x_mate)]
    near.append(push(gate_ref, gt_g.at[:, slot[1], :], seq=x_mate))
    for h in range(heads):
        late_f[h] = ge_ref[h, edge:, :]
        gd_g[h, :rows, :] = gated_ref[h]
        gt_g[h, :rows, :] = gate_ref[h]
    edge_copy.wait()
    has_next = jnp.where(s == seqs - 1, 0.0, 1.0)
    for h in range(heads):
        late_f[h, rows - edge :, :] += edge_in[h, :edge, :] * has_next
        lt_g[h, :rows, :] = late_f[h].astype(jnp.bfloat16)
    part = ab_ref[...]
    columns = mixer + values
    for h in range(heads):
        at = h * columns + mixer
        part = part + dot(gate_ref[h], w_ref[:, at : at + values], 1, 1)
    late_far = push(lt_g.at[:, slot[0], :], lt_g.at[:, slot[2], :], seq=z_mate)
    late_near = push(lt_g.at[:, slot[0], :], lt_g.at[:, slot[1], :], seq=x_mate)
    mid_copies = gather_columns(mid_t_ref, mid_g)
    one_copies = gather_columns(one_t_ref, one_g)
    rows_copies = []
    for k in range(1, seqs):
        to = lax.rem(s + k, seqs)
        block = pl.ds(pl.multiple_of(to * share, share), share)
        rows_copies.append(push(rows_ref.at[:, block], rows_in.at[s], seq=to))
    rows_in[s] = rows_ref[:, pl.ds(pl.multiple_of(s * share, share), share)]
    for h in range(heads):
        at = h * columns
        part = part + dot(lt_g[h, :rows, :], w_ref[:, at : at + mixer], 1, 1)

    for step in range(tensors.bit_length() - 1):
        red_send[step] = part.astype(jnp.bfloat16)
        mate = turned(t, 1 << step)
        copy = push(red_send.at[step], red_in.at[step], tensor=mate)
        if step == 0:
            for c in og:
                c.wait()
            total = og_in[0]
            for k in range(1, tensors):
                total = total + og_in[k]
            pack_own[: total.shape[0], :] = total
            pack_own[total.shape[0] :, :] = pack_ref[...]
            for c in far:
                c.wait()
            far_on = [
                push(gd_g.at[:, slot[2], :], gd_g.at[:, slot[3], :], seq=x_mate),
                push(gt_g.at[:, slot[2], :], gt_g.at[:, slot[3], :], seq=x_mate),
            ]
        else:
            late_far.wait()
            late_on = push(lt_g.at[:, slot[2], :], lt_g.at[:, slot[3], :], seq=x_mate)
            pack_copies = [
                push(pack_own, pack_in.at[s], seq=lax.rem(s + k, seqs)) for k in range(1, seqs)
            ]
            pack_in[s] = pack_own[...]
        copy.wait()
        part = red_send[step].astype(jnp.float32) + red_in[step].astype(jnp.float32)

    stream = hidden_ref[...].astype(jnp.float32)
    gain = gain_ref[...]
    inv = lax.rsqrt(jnp.mean(stream * stream, axis=-1, keepdims=True) + EPSILON)
    scaled = part * gain
    grad_out[...] = (
        middle_ref[...] + inv * scaled
        - stream * (inv * inv * inv) * jnp.mean(scaled * stream, axis=-1, keepdims=True)
    )
    gain_part = (part * stream * inv).reshape(rows // 8, 8, stream.shape[1])
    norm_send[...] = jnp.sum(gain_part, axis=0)

    exchanged = []

    def halves(copies, sources, left, block, width, at):
        for c in copies:
            c.wait()
        for h in range(heads):
            product = dot(left[...], block[h], 1, 0)
            cols = slice(at + h * width, at + (h + 1) * width)
            part_own[:, cols] = product[:share]
            part_send[:, cols] = product[share:].astype(jnp.bfloat16)
        cols = pl.ds(at, heads * width)
        exchanged.append(push(part_send.at[:, cols], part_in.at[:, cols], seq=turned(s, 4)))

    halves(mid_copies + [near[0], far_on[0]], None, mid_g, gd_g, values, 0)
    halves(one_copies + [near[1], far_on[1]], None, one_g, gt_g, values, heads * values)
    norm_copies = []
    for k in range(1, seqs):
        to = lax.rem(s + k, seqs)
        block = pl.ds(pl.multiple_of(to * share, share), share)
        norm_copies.append(push(norm_send.at[:, block], norm_in.at[s], seq=to))
    norm_in[s] = norm_send[:, pl.ds(pl.multiple_of(s * share, share), share)]
    halves([late_near, late_on], None, one_g, lt_g, mixer, 2 * heads * values)

    for c in rows_copies:
        c.wait()
    for c in pack_copies:
        c.wait()
    for ref, out in ((rows_in, rows_out), (pack_in, pack_out)):
        total = ref[0]
        for k in range(1, seqs):
            total = total + ref[k]
        out[...] = total
    for c in norm_copies:
        c.wait()
    total = norm_in[0]
    for k in range(1, seqs):
        total = total + norm_in[k]
    norm_out[...] = jnp.sum(total, axis=0, keepdims=True)

    def finish(copy, at, width, out, first):
        copy.wait()
        for h in range(heads):
            cols = slice(at + h * width, at + (h + 1) * width)
            out[:, h, first : first + width] = part_own[:, cols] + part_in[:, cols].astype(
                jnp.float32
            )

    finish(exchanged[0], 0, values, out_out, 0)
    finish(exchanged[1], heads * values, values, in_out, mixer)
    finish(exchanged[2], 2 * heads * values, mixer, in_out, 0)


def tail(ge, gate, gated, one_t, mid_t, w, ab, hidden, gain, middle, rows_small, pack, out_gain):
    heads, _, mixer = ge.shape
    _, rows, values = gated.shape
    model = hidden.shape[1]
    seqs, tensors = lax.axis_size("seq"), lax.axis_size("tensor")
    share = model // seqs
    wide_cols = heads * (mixer + 2 * values)
    joined_rows = pack.shape[0] + out_gain.shape[0]
    copies = 64
    bf16, f = jnp.bfloat16, jnp.float32
    return pl.pallas_call(
        tail_kernel,
        out_shape=(
            f32(share, heads, mixer + values),
            f32(share, heads, values),
            f32(rows, model),
            f32(rows_small.shape[0], share),
            f32(1, share),
            f32(joined_rows, pack.shape[1]),
        ),
        in_specs=[pl.BlockSpec(memory_space=pltpu.VMEM)] * 13,
        out_specs=tuple([pl.BlockSpec(memory_space=pltpu.VMEM)] * 6),
        scratch_shapes=[
            pltpu.VMEM((heads, 8, mixer), f),
            pltpu.VMEM((heads, rows, mixer), f),
            pltpu.VMEM((heads, 4 * rows, values), bf16),
            pltpu.VMEM((heads, 4 * rows, values), bf16),
            pltpu.VMEM((heads, 4 * rows, mixer), bf16),
            pltpu.VMEM((2 * share, 4 * rows), bf16),
            pltpu.VMEM((2 * share, 4 * rows), bf16),
            pltpu.VMEM((share, wide_cols), f),
            pltpu.VMEM((share, wide_cols), bf16),
            pltpu.VMEM((share, wide_cols), bf16),
            pltpu.VMEM((2, rows, model), bf16),
            pltpu.VMEM((2, rows, model), bf16),
            pltpu.VMEM((seqs, rows_small.shape[0], share), f),
            pltpu.VMEM((8, model), f),
            pltpu.VMEM((seqs, 8, share), f),
            pltpu.VMEM((seqs, joined_rows, pack.shape[1]), f),
            pltpu.VMEM((joined_rows, pack.shape[1]), f),
            pltpu.VMEM((tensors, *out_gain.shape), f),
            pltpu.SemaphoreType.DMA((copies,)),
            pltpu.SemaphoreType.DMA((copies,)),
        ],
        compiler_params=pltpu.CompilerParams(collective_id=0, has_side_effects=True),
        name="tail",
    )(ge, gate, gated, one_t, mid_t, w, ab, hidden, gain, middle, rows_small, pack, out_gain)


def shards(
    hidden_in,
    seq_ids,
    norm_gain,
    w_in,
    w_ab,
    conv_w,
    a_log,
    dt_bias,
    out_gain,
    w_out,
    ffn_gain,
    w_gu,
    w_down,
    out_grad,
):
    row_count, model = hidden_in.shape
    heads = w_in.shape[1]
    width = conv_w.shape[1]
    mixer_width = conv_w.shape[2]
    count = lax.axis_size("seq")
    here = lax.axis_index("seq")
    first_row = here * row_count
    padded_ids = jnp.concatenate([jnp.full((width - 1,), -1, jnp.int32), seq_ids])
    ids_ext = lax.dynamic_slice_in_dim(padded_ids, first_row, row_count + width - 1)
    own_ids = ids_ext[width - 1 :]
    ids_row = own_ids.astype(jnp.float32)[None, :]
    same_first = (own_ids == ids_ext[width - 2]).astype(jnp.float32)[None, :]
    stream = hidden_in.astype(jnp.float32)
    normed_f, inv_one = rms_forward(stream, norm_gain)
    normed_one = normed_f.astype(jnp.bfloat16)
    projected = bf(
        jnp.einsum("td,dhp->htp", normed_one, w_in, preferred_element_type=jnp.float32)
    )
    mixer_ab = jnp.einsum("td,dhc->hct", normed_one, w_ab, preferred_element_type=jnp.float32)
    mixer_cols = projected[:, :, :mixer_width]
    edge_rows = passed_along(mixer_cols[:, row_count - width + 1 :], "seq", 1)
    extended = wide(jnp.concatenate([edge_rows, mixer_cols], axis=1))
    gate_in = wide(projected[:, :, mixer_width:])

    def prepare_local(ext_in, decay_in, rate_in, conv_in, alog_in, bias_in):
        return prepare(ext_in, decay_in, rate_in, conv_in, alog_in, bias_in, ids_ext)

    prepared, prepare_back = jax.vjp(
        prepare_local, extended, mixer_ab[:, 0], mixer_ab[:, 1], conv_w, a_log, dt_bias
    )
    share = model // count
    blocked = share % 128 == 0
    squared = blocked and count == 2 * 4 and lax.axis_size("tensor") == 4
    if squared:
        inverse, fresh, query_eff, reading, state_in, maps = mixer_forward(
            *prepared, ids_row, same_first
        )
    else:
        inverse, fresh, readings, carry = delta_forward(*prepared, ids_row, same_first)
        query_eff = readings[:, :, :DK]
        state_in, maps = state_before(carry)
        reading = readings[:, :, DK:] + bmm(query_eff, state_in)
    gated_f, gate_back = jax.vjp(output_gate, reading, gate_in, out_gain)
    gated = bf(gated_f)
    mixed_part = jnp.einsum("hte,dhe->td", gated, w_out, preferred_element_type=jnp.float32)
    mixed = exchanged_sum(mixed_part, "tensor", jnp.bfloat16)
    if not squared:
        mixed, maps = lax.optimization_barrier((mixed, maps))
    middle = stream + mixed
    normed_two_f, inv_two = rms_forward(middle, ffn_gain)
    normed_two = bf(normed_two_f)
    gate_part = jnp.dot(normed_two, w_gu[:, 0], preferred_element_type=jnp.float32)
    up_part = jnp.dot(normed_two, w_gu[:, 1], preferred_element_type=jnp.float32)
    hidden_ffn = bf(jax.nn.silu(gate_part) * up_part)
    ffn_part = jnp.einsum("tf,df->td", hidden_ffn, w_down, preferred_element_type=jnp.float32)
    ffn_out = exchanged_sum(ffn_part, "tensor", jnp.bfloat16)
    block_out = bf(middle + ffn_out)
    grad_top = wide(out_grad)
    grad_hidden = jnp.dot(out_grad, w_down, preferred_element_type=jnp.float32)
    sigmoid_gate = jax.nn.sigmoid(gate_part)
    grad_gate_ffn = bf(
        grad_hidden * up_part * sigmoid_gate * (1.0 + gate_part * (1.0 - sigmoid_gate))
    )
    grad_up = bf(grad_hidden * gate_part * sigmoid_gate)
    normed_two_part = jnp.einsum(
        "tf,df->td", grad_gate_ffn, w_gu[:, 0], preferred_element_type=jnp.float32
    ) + jnp.einsum("tf,df->td", grad_up, w_gu[:, 1], preferred_element_type=jnp.float32)
    grad_normed_two = exchanged_sum(normed_two_part, "tensor", jnp.bfloat16)
    ffn_width = w_down.shape[1]
    if blocked:
        ffn_grads = ffn_products(normed_two, out_grad, grad_gate_ffn, grad_up, hidden_ffn, count)
        ffn_share = wide(lax.psum_scatter(ffn_grads, "seq", scatter_dimension=0, tiled=True))
        share_w_gu = ffn_share[: 2 * ffn_width].reshape(2, ffn_width, share).transpose(2, 0, 1)
        share_w_down = ffn_share[2 * ffn_width :].T
    else:
        ffn_grads = jnp.concatenate(
            [
                bf(jnp.einsum("td,tf->df", normed_two, grad_gate_ffn, preferred_element_type=jnp.float32)),
                bf(jnp.einsum("td,tf->df", normed_two, grad_up, preferred_element_type=jnp.float32)),
                bf(jnp.einsum("td,tf->df", out_grad, hidden_ffn, preferred_element_type=jnp.float32)),
            ],
            axis=1,
        )
        ffn_share = wide(lax.psum_scatter(ffn_grads, "seq", scatter_dimension=0, tiled=True))
        share_w_gu = ffn_share[:, : 2 * ffn_width].reshape(-1, 2, ffn_width)
        share_w_down = ffn_share[:, 2 * ffn_width :]
    grad_middle_norm, grad_ffn_gain = rms_backward(middle, inv_two, ffn_gain, grad_normed_two)
    grad_middle = grad_top + grad_middle_norm
    grad_middle_b = bf(grad_middle)
    grad_gated = jnp.einsum("td,dhe->hte", grad_middle_b, w_out, preferred_element_type=jnp.float32)
    grad_reading, grad_gate_in, gain_part = gate_back(grad_gated)
    if squared:
        delta_grads = mixer_backward(
            *prepared, ids_row, same_first, inverse, fresh, query_eff, state_in, maps, grad_reading
        )
    else:
        carry_grad = jnp.einsum("htd,hte->hde", query_eff, grad_reading, precision=PRECISE)
        state_grad = grad_after(carry_grad, maps)
        delta_grads = delta_backward(
            *prepared, ids_row, same_first, inverse, fresh, state_in, grad_reading, state_grad
        )
    grad_extended, grad_decay, grad_rate, grad_conv_w, grad_a_log, grad_dt_bias = prepare_back(
        tuple(delta_grads)
    )
    grad_ab_b = bf(jnp.stack([grad_decay, grad_rate], axis=1))
    grad_w_ab = jnp.einsum(
        "td,hct->hcd", normed_one, grad_ab_b, preferred_element_type=jnp.float32
    )
    ab_part = jnp.einsum("hct,dhc->td", grad_ab_b, w_ab, preferred_element_type=jnp.float32)
    if squared:
        rows_small = jnp.concatenate(
            [grad_ffn_gain[None], grad_w_ab.reshape(2 * heads, model)], axis=0
        )
        rows_small = jnp.pad(rows_small, ((0, -rows_small.shape[0] % 8), (0, 0)))
        packed = jnp.concatenate([part.reshape(-1) for part in (grad_conv_w, grad_a_log, grad_dt_bias)])
        packed = jnp.pad(packed, (0, -packed.shape[0] % 1024)).reshape(-1, 128)
        gain_rows = jnp.pad(gain_part, (0, -gain_part.shape[0] % 1024)).reshape(-1, 128)
        share_w_in, share_w_out, grad_in, rows_sum, norm_gain_own, pack_sum = tail(
            grad_extended, bf(grad_gate_in), gated, normed_one.T, grad_middle_b.T,
            w_in.reshape(model, -1), ab_part, hidden_in, norm_gain[None], grad_middle,
            rows_small, packed, gain_rows,
        )
        flat = pack_sum.reshape(-1)
        at = gain_rows.size
        conv_end = at + grad_conv_w.size
        return (
            block_out,
            grad_in,
            norm_gain_own[0],
            share_w_in,
            jnp.transpose(rows_sum[1 : 1 + 2 * heads].reshape(heads, 2, share), (2, 0, 1)),
            flat[at:conv_end].reshape(grad_conv_w.shape),
            flat[conv_end : conv_end + heads],
            flat[conv_end + heads : conv_end + 2 * heads],
            flat[: gain_part.shape[0]],
            share_w_out,
            rows_sum[0],
            share_w_gu,
            share_w_down,
        )
    returned_edge = passed_along(grad_extended[:, : width - 1], "seq", -1)
    grad_mixer = jnp.concatenate(
        [
            grad_extended[:, width - 1 : row_count],
            grad_extended[:, row_count:] + returned_edge,
        ],
        axis=1,
    )
    grad_projected = bf(jnp.concatenate([grad_mixer, grad_gate_in], axis=-1))
    w_out_grad = jnp.einsum(
        "td,hte->dhe", grad_middle_b, gated, preferred_element_type=jnp.float32
    )
    w_in_grad = jnp.einsum(
        "td,htp->dhp", normed_one, grad_projected, preferred_element_type=jnp.float32
    )
    mixer_grads = jnp.concatenate(
        [bf(w_in_grad).reshape(model, -1), bf(w_out_grad).reshape(model, -1)], axis=1
    )
    mixer_share = wide(lax.psum_scatter(mixer_grads, "seq", scatter_dimension=0, tiled=True))
    in_width = heads * w_in.shape[2]
    share_w_in = mixer_share[:, :in_width].reshape(-1, heads, w_in.shape[2])
    share_w_out = mixer_share[:, in_width:].reshape(-1, heads, w_out.shape[2])
    normed_one_part = jnp.einsum(
        "htp,dhp->td", grad_projected, w_in, preferred_element_type=jnp.float32
    )
    normed_one_part = normed_one_part + ab_part
    grad_normed_one = exchanged_sum(normed_one_part, "tensor", jnp.bfloat16)
    gain_total = exchanged_sum(gain_part, "tensor", jnp.float32)
    grad_norm_in, grad_norm_gain = rms_backward(stream, inv_one, norm_gain, grad_normed_one)
    grad_in = grad_middle + grad_norm_in
    parts = (
        grad_conv_w, gain_total, grad_ffn_gain, grad_norm_gain, grad_w_ab, grad_a_log, grad_dt_bias,
    )
    packed = jnp.concatenate([part.reshape(-1) for part in parts])
    length = packed.shape[0]
    packed = jnp.pad(packed, (0, -length % 1024)).reshape(-1, 128)
    total = exchanged_sum(packed, "seq", jnp.float32).reshape(-1)
    pieces, at = [], 0
    for part in parts:
        pieces.append(total[at : at + part.size].reshape(part.shape))
        at += part.size
    conv_sum, gain_sum, ffn_gain_sum, norm_gain_sum, w_ab_sum, a_log_sum, dt_bias_sum = pieces
    def own(whole, dim):
        return lax.dynamic_slice_in_dim(whole, here * share, share, dim)

    return (
        block_out,
        grad_in,
        own(norm_gain_sum, 0),
        share_w_in,
        jnp.transpose(own(w_ab_sum, 2), (2, 0, 1)),
        conv_sum,
        a_log_sum,
        dt_bias_sum,
        gain_sum,
        share_w_out,
        own(ffn_gain_sum, 0),
        share_w_gu,
        share_w_down,
    )


def solution(mesh):
    return jax.shard_map(
        shards,
        mesh=mesh,
        in_specs=(
            P("seq", None),
            P(),
            P(),
            P(None, "tensor", None),
            P(None, "tensor", None),
            P("tensor", None, None),
            P("tensor"),
            P("tensor"),
            P(),
            P(None, "tensor", None),
            P(),
            P(None, None, "tensor"),
            P(None, "tensor"),
            P("seq", None),
        ),
        out_specs=(
            P("seq", None),
            P("seq", None),
            P("seq"),
            P("seq", "tensor", None),
            P("seq", "tensor", None),
            P("tensor", None, None),
            P("tensor"),
            P("tensor"),
            P(),
            P("seq", "tensor", None),
            P("seq"),
            P("seq", None, "tensor"),
            P("seq", "tensor"),
        ),
        check_vma=False,
    )
```

```python
import math

import jax
import jax.numpy as jnp
from jax import lax
from jax.experimental import pallas as pl
from jax.experimental.pallas import tpu as pltpu
from jax.sharding import PartitionSpec as P

DK = 128

EPSILON = 1e-06
PRECISE = lax.Precision.HIGHEST


def passed_along(block, axis, distance):
    devices = range(lax.axis_size(axis))
    route = [(i - distance, i) for i in devices if i - distance in devices]
    return lax.ppermute(block, axis, route)


def exchanged_sum(part, axis, kind):
    count = lax.axis_size(axis)
    if count & (count - 1):
        return lax.psum(part.astype(kind), axis).astype(jnp.float32)
    distance = 1
    while distance < count:
        own = part.astype(kind)
        other = lax.ppermute(own, axis, [(i, i ^ distance) for i in range(count)])
        part = own.astype(jnp.float32) + other.astype(jnp.float32)
        distance *= 2
    return part


def bf(x):
    return x.astype(jnp.bfloat16)


def wide(x):
    return x.astype(jnp.float32)


def bmm(a, b):
    return jnp.einsum("hab,hbe->hae", a, b, precision=PRECISE)


def rms_forward(values_in, gain):
    inv_scale = lax.rsqrt(jnp.mean(values_in * values_in, axis=-1, keepdims=True) + EPSILON)
    return (values_in * inv_scale * gain, inv_scale)


def rms_backward(values_in, inv_scale, gain, upstream):
    scaled = upstream * gain
    cubed = inv_scale * inv_scale * inv_scale
    result_grad = inv_scale * scaled - values_in * cubed * jnp.mean(
        scaled * values_in, axis=-1, keepdims=True
    )
    gain_grad = jnp.sum(upstream * values_in * inv_scale, axis=0)
    return (result_grad, gain_grad)


def prepare(extended, decay_in, rate_in, conv_w, a_log, dt_bias, ids_ext):
    width = conv_w.shape[1]
    row_count = decay_in.shape[1]
    current = ids_ext[width - 1 :]
    conv_sum = 0.0
    for offset in range(width):
        same_seq = (ids_ext[offset : offset + row_count] == current).astype(jnp.float32)
        conv_sum = (
            conv_sum
            + extended[:, offset : offset + row_count]
            * conv_w[:, offset, :][:, None, :]
            * same_seq[None, :, None]
        )
    activated = jax.nn.silu(conv_sum)
    q_raw = activated[:, :, :DK]
    k_raw = activated[:, :, DK : 2 * DK]
    values = activated[:, :, 2 * DK :]
    queries = (
        q_raw
        * lax.rsqrt(jnp.sum(q_raw * q_raw, axis=-1, keepdims=True) + EPSILON)
        * (1.0 / math.sqrt(DK))
    )
    key_vecs = k_raw * lax.rsqrt(jnp.sum(k_raw * k_raw, axis=-1, keepdims=True) + EPSILON)
    write_rate = jax.nn.sigmoid(rate_in)
    log_decay = -jnp.exp(a_log)[:, None] * jax.nn.softplus(decay_in + dt_bias[:, None])
    return (queries, key_vecs, values, write_rate, log_decay)


def mm(a, b, ca, cb):
    return lax.dot_general(
        a, b, (((ca,), (cb,)), ((), ())), precision=PRECISE, preferred_element_type=jnp.float32
    )


def grids(rows):
    i = lax.broadcasted_iota(jnp.int32, (rows, rows), 0)
    j = lax.broadcasted_iota(jnp.int32, (rows, rows), 1)
    return i, j


def as_col(row, eye):
    return jnp.sum(jnp.where(eye, row, 0.0), axis=1, keepdims=True)


def as_row(col, eye):
    return jnp.sum(jnp.where(eye, col, 0.0), axis=0, keepdims=True)


def block_terms(g_row, b_row, ids_row, first_row, i, j):
    eye = i == j
    g_col = as_col(g_row, eye)
    cum_col = jnp.sum(jnp.where(i >= j, g_row, 0.0), axis=1, keepdims=True)
    cum_row = jnp.sum(jnp.where(i <= j, g_col, 0.0), axis=0, keepdims=True)
    allowed = (i >= j) & (as_col(ids_row, eye) == ids_row)
    weights = jnp.where(allowed, jnp.exp(jnp.minimum(cum_col - cum_row, 0.0)), 0.0)
    from_start = as_col(first_row, eye) * jnp.exp(cum_col)
    return weights, from_start, as_col(b_row, eye)


def delta_forward_kernel(
    q_ref, k_ref, v_ref, b_ref, g_ref, ids_ref, first_ref, inv_ref, f_ref, r_ref, s_ref
):
    heads, rows, _ = q_ref.shape
    i, j = grids(rows)
    eye = i == j
    keep = []
    for h in range(heads):
        weights, from_start, b_col = block_terms(
            g_ref[h : h + 1, :], b_ref[h : h + 1, :], ids_ref[...], first_ref[...], i, j
        )
        k = k_ref[h]
        lower = jnp.where(i > j, weights * mm(k, k, 1, 1) * b_col, 0.0)
        keep.append((weights, from_start, b_col, lower))
    inverses = [jnp.where(eye, 1.0, 0.0)] * heads
    size = 1
    while size < rows:
        pair = (i // (2 * size) == j // (2 * size)) & (i // size > j // size)
        for h in range(heads):
            off = jnp.where(pair, keep[h][3], 0.0)
            if size > 1:
                off = mm(mm(inverses[h], off, 1, 0), inverses[h], 1, 0)
            inverses[h] = inverses[h] - off
        size *= 2
    for h in range(heads):
        weights, from_start, b_col, _ = keep[h]
        q, k, v = q_ref[h], k_ref[h], v_ref[h]
        target = jnp.concatenate([-(b_col * from_start) * k, b_col * v], axis=1)
        fresh = mm(inverses[h], target, 1, 0)
        query_key = mm(q, k, 1, 1) * weights
        reading = mm(query_key, fresh, 1, 0)
        last = as_col(weights[rows - 1 :, :], eye)
        state = mm(k * last, fresh, 0, 0)
        inv_ref[h] = inverses[h]
        f_ref[h] = fresh
        r_ref[h, :, :DK] = reading[:, :DK] + from_start * q
        r_ref[h, :, DK:] = reading[:, DK:]
        di, dj = grids(DK)
        own_map = state[:, :DK] + jnp.where(di == dj, from_start[rows - 1 :, :], 0.0)
        s_ref[h, :, :DK] = own_map.astype(s_ref.dtype)
        s_ref[h, :, DK:] = state[:, DK:].astype(s_ref.dtype)


def delta_backward_kernel(
    q_ref, k_ref, v_ref, b_ref, g_ref, ids_ref, first_ref, inv_ref, f_ref,
    s_ref, dr_ref, ds_ref, dq_ref, dk_ref, dv_ref, db_ref, dg_ref,
):
    heads, rows, _ = q_ref.shape
    i, j = grids(rows)
    eye = i == j
    for h in range(heads):
        weights, from_start, b_col = block_terms(
            g_ref[h : h + 1, :], b_ref[h : h + 1, :], ids_ref[...], first_ref[...], i, j
        )
        q, k, v = q_ref[h], k_ref[h], v_ref[h]
        state, d_read, d_state = s_ref[h], dr_ref[h], ds_ref[h]
        fresh = f_ref[h, :, DK:] + mm(f_ref[h, :, :DK], state, 1, 0)
        qk = mm(q, k, 1, 1)
        kk = mm(k, k, 1, 1)
        q_state = mm(q, state, 1, 0)
        k_state = mm(k, state, 1, 0)
        last = as_col(weights[rows - 1 :, :], eye)
        d_fresh = mm(qk * weights, d_read, 0, 0) + mm(k * last, d_state, 1, 0)
        d_target = mm(inv_ref[h], d_fresh, 0, 0)
        d_lower = jnp.where(i > j, -mm(d_target, fresh, 1, 1), 0.0)
        d_p = mm(d_read, fresh, 1, 1)
        d_qk = d_p * weights
        d_kk = d_lower * weights * b_col
        d_klast = mm(fresh, d_state, 1, 1)
        d_last = as_row(jnp.sum(d_klast * k, axis=1, keepdims=True), eye)
        d_w = d_p * qk + d_lower * kk * b_col + jnp.where(i == rows - 1, d_last, 0.0)
        dq_ref[h] = mm(from_start * d_read, state, 1, 1) + mm(d_qk, k, 1, 0)
        dk_ref[h] = (
            mm(-(b_col * from_start) * d_target, state, 1, 1)
            + mm(d_qk, q, 0, 0)
            + mm(d_kk, k, 1, 0)
            + mm(d_kk, k, 0, 0)
            + last * d_klast
        )
        dv_ref[h] = b_col * d_target
        d_b = jnp.sum(d_target * (v - from_start * k_state), axis=1, keepdims=True) + jnp.sum(
            d_lower * weights * kk, axis=1, keepdims=True
        )
        d_fs = jnp.sum(d_read * q_state - b_col * d_target * k_state, axis=1, keepdims=True)
        d_fs_last = jnp.sum(
            jnp.sum(d_state * state, axis=1, keepdims=True), axis=0, keepdims=True
        )
        at_end = lax.broadcasted_iota(jnp.int32, (rows, 1), 0) == rows - 1
        d_fs = d_fs + jnp.where(at_end, d_fs_last, 0.0)
        spread = d_w * weights
        d_cum = (
            jnp.sum(spread, axis=1, keepdims=True)
            - as_col(jnp.sum(spread, axis=0, keepdims=True), eye)
            + d_fs * from_start
        )
        db_ref[h : h + 1, :] = as_row(d_b, eye)
        dg_ref[h : h + 1, :] = jnp.sum(jnp.where(i >= j, d_cum, 0.0), axis=0, keepdims=True)


def f32(*shape):
    return jax.ShapeDtypeStruct(shape, jnp.float32)


def delta_forward(q, k, v, b, g, ids_row, first_row):
    heads, rows, _ = q.shape
    joined = DK + v.shape[2]
    return pl.pallas_call(
        delta_forward_kernel,
        out_shape=(
            f32(heads, rows, rows),
            f32(heads, rows, joined),
            f32(heads, rows, joined),
            jax.ShapeDtypeStruct((heads, DK, joined), jnp.bfloat16),
        ),
        name="delta_forward",
    )(q, k, v, b, g, ids_row, first_row)


def delta_backward(q, k, v, b, g, ids_row, first_row, inv, fresh, state, d_read, d_state):
    return pl.pallas_call(
        delta_backward_kernel,
        out_shape=(
            f32(*q.shape), f32(*k.shape), f32(*v.shape), f32(*b.shape), f32(*g.shape),
        ),
        name="delta_backward",
    )(q, k, v, b, g, ids_row, first_row, inv, fresh, state, d_read, d_state)


def output_gate(reading, gate_in, out_gain):
    inv_scale = lax.rsqrt(jnp.mean(reading * reading, axis=-1, keepdims=True) + EPSILON)
    return reading * inv_scale * out_gain * jax.nn.silu(gate_in)


def spans(count):
    found, span = [], 2
    while span < count - 1:
        found.append(span)
        span *= 2
    return found


def state_before(carry):
    first = wide(passed_along(carry, "seq", 1))
    second = wide(passed_along(carry, "seq", 2))
    moved = bmm(first[:, :, :DK], second)
    held_map, held_add = moved[:, :, :DK], first[:, :, DK:] + moved[:, :, DK:]
    found = [(1, carry[:, :, :DK])]
    steps = spans(lax.axis_size("seq"))
    for span in steps:
        found.append((span, bf(held_map)))
        if span == steps[-1]:
            held_add = held_add + bmm(held_map, wide(passed_along(bf(held_add), "seq", span)))
        else:
            sent = bf(jnp.concatenate([held_map, held_add], axis=-1))
            moved = bmm(held_map, wide(passed_along(sent, "seq", span)))
            held_map, held_add = moved[:, :, :DK], held_add + moved[:, :, DK:]
    maps = []
    for span, block in found:
        back = 1 if span == 1 else span + 1
        maps.append(passed_along(block, "seq", -back))
    return held_add, maps


def grad_after(carry_grad, maps):
    own = bf(carry_grad)
    flipped = [jnp.swapaxes(wide(block), 1, 2) for block in maps]
    first = wide(passed_along(own, "seq", -1))
    held = first + bmm(flipped[0], wide(passed_along(own, "seq", -2)))
    for span, here in zip(spans(lax.axis_size("seq")), flipped[1:]):
        held = held + bmm(here, wide(passed_along(bf(held), "seq", -span)))
    return held


def bdot(a, b, ca, cb):
    return bf(
        lax.dot_general(a, b, (((ca,), (cb,)), ((), ())), preferred_element_type=jnp.float32)
    )


def turned(index, bit):
    return index + bit * (1 - 2 * ((index // bit) % 2))


def send(src, dst, sends, receives, at, where):
    copy = pltpu.make_async_remote_copy(
        src_ref=src,
        dst_ref=dst,
        send_sem=sends.at[at],
        recv_sem=receives.at[at],
        device_id=where,
        device_id_type=pl.DeviceIdType.MESH,
    )
    copy.start()
    return copy


def greet(axis_counts):
    barrier = pltpu.get_barrier_semaphore()
    total = 0
    for axis, count in axis_counts:
        me = lax.axis_index(axis)
        for k in range(1, count):
            pl.semaphore_signal(
                barrier, inc=1, device_id={axis: lax.rem(me + k, count)},
                device_id_type=pl.DeviceIdType.MESH,
            )
        total += count - 1
    pl.semaphore_wait(barrier, total)


def dot(a, b, ca, cb):
    return lax.dot_general(a, b, (((ca,), (cb,)), ((), ())), preferred_element_type=jnp.float32)


def greet_line():
    seqs = lax.axis_size("seq")
    s = lax.axis_index("seq")
    z, last = s // 2, seqs // 2 - 1
    barrier = pltpu.get_barrier_semaphore()

    def hail(where):
        pl.semaphore_signal(
            barrier, inc=1, device_id={"seq": where}, device_id_type=pl.DeviceIdType.MESH
        )

    hail(turned(s, 1))

    @pl.when(z > 0)
    def _():
        hail(s - 2)

    @pl.when(z < last)
    def _():
        hail(s + 2)

    pl.semaphore_wait(barrier, 1 + (z + last) // (last + 1) + (2 * last - z) // (last + 1))


def remote(src, dst, sends, receives, at, where):
    return pltpu.make_async_remote_copy(
        src_ref=src,
        dst_ref=dst,
        send_sem=sends.at[at],
        recv_sem=receives.at[at],
        device_id={"seq": where},
        device_id_type=pl.DeviceIdType.MESH,
    )


def mixer_forward_kernel(
    q_ref, k_ref, v_ref, b_ref, g_ref, ids_ref, first_ref,
    inv_ref, f_ref, eff_ref, r_ref, state_ref, map_ref,
    carry, mate, onward, arrived, sends, receives,
):
    heads, rows, _ = q_ref.shape
    s = lax.axis_index("seq")
    z, last = s // 2, lax.axis_size("seq") // 2 - 1
    lane = s % 2
    greet_line()
    i, j = grids(rows)
    eye = i == j
    keep = []
    for h in range(heads):
        weights, from_start, b_col = block_terms(
            g_ref[h : h + 1, :], b_ref[h : h + 1, :], ids_ref[...], first_ref[...], i, j
        )
        k = k_ref[h]
        lower = jnp.where(i > j, weights * mm(k, k, 1, 1) * b_col, 0.0)
        keep.append((weights, from_start, b_col, lower))
    inverses = [jnp.where(eye, 1.0, 0.0)] * heads
    size = 1
    while size < rows:
        pair = (i // (2 * size) == j // (2 * size)) & (i // size > j // size)
        for h in range(heads):
            off = jnp.where(pair, keep[h][3], 0.0)
            if size > 1:
                off = mm(mm(inverses[h], off, 1, 0), inverses[h], 1, 0)
            inverses[h] = inverses[h] - off
        size *= 2
    freshes, swaps = [], []
    di, dj = grids(DK)
    for h in range(heads):
        weights, from_start, b_col, _ = keep[h]
        k, v = k_ref[h], v_ref[h]
        target = jnp.concatenate([-(b_col * from_start) * k, b_col * v], axis=1)
        fresh = mm(inverses[h], target, 1, 0)
        end = as_col(weights[rows - 1 :, :], eye)
        state = mm(k * end, fresh, 0, 0)
        own_map = state[:, :DK] + jnp.where(di == dj, from_start[rows - 1 :, :], 0.0)
        carry[h, :, :DK] = bf(own_map)
        carry[h, :, DK:] = bf(state[:, DK:])
        freshes.append(fresh)
        swap = remote(carry.at[h], mate.at[h], sends, receives, h, turned(s, 1))
        swap.start()
        swaps.append(swap)

    @pl.when(z == 0)
    def _():
        arrived[...] = jnp.zeros_like(arrived)

    for h in range(heads):
        weights, from_start, _, _ = keep[h]
        q = q_ref[h]
        reading = mm(mm(q, k_ref[h], 1, 1) * weights, freshes[h], 1, 0)
        inv_ref[h] = inverses[h]
        f_ref[h] = freshes[h]
        eff_ref[h] = reading[:, :DK] + from_start * q
        r_ref[h] = reading[:, DK:]
    adds = []
    for h in range(heads):
        swaps[h].wait()
        own, other = wide(carry[h]), wide(mate[h])
        one = jnp.where(lane == 0, own, other)
        two = jnp.where(lane == 0, other, own)
        joined = mm(two[:, :DK], one, 1, 0)
        map_ref[0, h] = one[:, :DK]
        map_ref[1, h] = two[:, :DK]
        map_ref[2, h] = joined[:, :DK]
        adds.append((one[:, DK:], joined[:, DK:] + two[:, DK:]))
    hops = [
        remote(onward.at[h], arrived.at[h], sends, receives, heads + h, lax.rem(s + 2, 2 * last + 2))
        for h in range(heads)
    ]
    for h in range(heads):

        @pl.when(z > 0)
        def _():
            hops[h].wait_recv()

        held = wide(arrived[h])

        @pl.when(z < last)
        def _():
            onward[h] = bf(adds[h][1] + mm(map_ref[2, h], held, 1, 0))
            hops[h].start()

        state_ref[h] = jnp.where(lane == 0, held, adds[h][0] + mm(map_ref[0, h], held, 1, 0))
    for h in range(heads):
        r_ref[h] += mm(eff_ref[h], state_ref[h], 1, 0)

        @pl.when(z < last)
        def _():
            hops[h].wait_send()


def mixer_forward(q, k, v, b, g, ids_row, first_row):
    heads, rows, _ = q.shape
    values = v.shape[2]
    bf16 = jnp.bfloat16
    return pl.pallas_call(
        mixer_forward_kernel,
        out_shape=(
            f32(heads, rows, rows),
            f32(heads, rows, DK + values),
            f32(heads, rows, DK),
            f32(heads, rows, values),
            f32(heads, DK, values),
            f32(3, heads, DK, DK),
        ),
        scratch_shapes=[
            pltpu.VMEM((heads, DK, DK + values), bf16),
            pltpu.VMEM((heads, DK, DK + values), bf16),
            pltpu.VMEM((heads, DK, values), bf16),
            pltpu.VMEM((heads, DK, values), bf16),
            pltpu.SemaphoreType.DMA((2 * heads,)),
            pltpu.SemaphoreType.DMA((2 * heads,)),
        ],
        compiler_params=pltpu.CompilerParams(collective_id=1, has_side_effects=True),
        name="mixer_forward",
    )(q, k, v, b, g, ids_row, first_row)


def mixer_backward_kernel(
    q_ref, k_ref, v_ref, b_ref, g_ref, ids_ref, first_ref, inv_ref, f_ref, eff_ref,
    s_ref, map_ref, dr_ref, block_ref, cols_ref,
    dq_ref, dk_ref, dv_ref, db_ref, dg_ref, own_ref, send_ref,
    carry, mate, onward, arrived, diagonal, sends, receives,
):
    heads, rows, _ = q_ref.shape
    s = lax.axis_index("seq")
    z, last = s // 2, lax.axis_size("seq") // 2 - 1
    lane = s % 2
    greet_line()
    swaps = []
    for h in range(heads):
        carry[h] = bf(mm(eff_ref[h], dr_ref[h], 0, 0))
        swap = remote(carry.at[h], mate.at[h], sends, receives, h, turned(s, 1))
        swap.start()
        swaps.append(swap)

    @pl.when(z == last)
    def _():
        arrived[...] = jnp.zeros_like(arrived)

    passes = []
    for k in range(3):
        far = block_ref.at[k, pl.ds(2 * rows, rows), :]
        passes.append(
            remote(far, diagonal.at[k], sends, receives, 2 * heads + k, turned(s, 1))
        )
        passes[k].start()
    i, j = grids(rows)
    eye = i == j
    early = []
    for h in range(heads):
        weights, from_start, b_col = block_terms(
            g_ref[h : h + 1, :], b_ref[h : h + 1, :], ids_ref[...], first_ref[...], i, j
        )
        q, k = q_ref[h], k_ref[h]
        state, d_read = s_ref[h], dr_ref[h]
        fresh = f_ref[h, :, DK:] + mm(f_ref[h, :, :DK], state, 1, 0)
        qk = mm(q, k, 1, 1)
        kk = mm(k, k, 1, 1)
        d_p = mm(d_read, fresh, 1, 1)
        d_fresh = mm(qk * weights, d_read, 0, 0)
        early.append((weights, from_start, b_col, fresh, qk, kk, d_p, d_fresh))
    firsts, joints = [], []
    for h in range(heads):
        swaps[h].wait()
        own, other = wide(carry[h]), wide(mate[h])
        one = jnp.where(lane == 0, own, other)
        two = jnp.where(lane == 0, other, own)
        firsts.append(two)
        joints.append(one + mm(map_ref[0, h], two, 0, 0))
    hops = [
        remote(
            onward.at[h], arrived.at[h], sends, receives, heads + h,
            lax.rem(s + 2 * last, 2 * last + 2),
        )
        for h in range(heads)
    ]
    for h in range(heads):

        @pl.when(z < last)
        def _():
            hops[h].wait_recv()

        held = wide(arrived[h])

        @pl.when(z > 0)
        def _():
            onward[h] = bf(joints[h] + mm(map_ref[2, h], held, 0, 0))
            hops[h].start()

        firsts[h] = jnp.where(lane == 1, held, firsts[h] + mm(map_ref[1, h], held, 0, 0))
    for h in range(heads):
        weights, from_start, b_col, fresh, qk, kk, d_p, d_fresh = early[h]
        q, k, v = q_ref[h], k_ref[h], v_ref[h]
        state, d_read, d_state = s_ref[h], dr_ref[h], firsts[h]
        q_state = mm(q, state, 1, 0)
        k_state = mm(k, state, 1, 0)
        end = as_col(weights[rows - 1 :, :], eye)
        d_fresh = d_fresh + mm(k * end, d_state, 1, 0)
        d_target = mm(inv_ref[h], d_fresh, 0, 0)
        d_lower = jnp.where(i > j, -mm(d_target, fresh, 1, 1), 0.0)
        d_qk = d_p * weights
        d_kk = d_lower * weights * b_col
        d_klast = mm(fresh, d_state, 1, 1)
        d_last = as_row(jnp.sum(d_klast * k, axis=1, keepdims=True), eye)
        d_w = d_p * qk + d_lower * kk * b_col + jnp.where(i == rows - 1, d_last, 0.0)
        dq_ref[h] = mm(from_start * d_read, state, 1, 1) + mm(d_qk, k, 1, 0)
        dk_ref[h] = (
            mm(-(b_col * from_start) * d_target, state, 1, 1)
            + mm(d_qk, q, 0, 0)
            + mm(d_kk, k, 1, 0)
            + mm(d_kk, k, 0, 0)
            + end * d_klast
        )
        dv_ref[h] = b_col * d_target
        d_b = jnp.sum(d_target * (v - from_start * k_state), axis=1, keepdims=True) + jnp.sum(
            d_lower * weights * kk, axis=1, keepdims=True
        )
        d_fs = jnp.sum(d_read * q_state - b_col * d_target * k_state, axis=1, keepdims=True)
        d_fs_last = jnp.sum(
            jnp.sum(d_state * state, axis=1, keepdims=True), axis=0, keepdims=True
        )
        at_end = lax.broadcasted_iota(jnp.int32, (rows, 1), 0) == rows - 1
        d_fs = d_fs + jnp.where(at_end, d_fs_last, 0.0)
        spread = d_w * weights
        d_cum = (
            jnp.sum(spread, axis=1, keepdims=True)
            - as_col(jnp.sum(spread, axis=0, keepdims=True), eye)
            + d_fs * from_start
        )
        db_ref[h : h + 1, :] = as_row(d_b, eye)
        dg_ref[h : h + 1, :] = jnp.sum(jnp.where(i >= j, d_cum, 0.0), axis=0, keepdims=True)

        @pl.when(z > 0)
        def _():
            hops[h].wait_send()

    share = own_ref.shape[1]
    for k in range(3):
        passes[k].wait()
        left = cols_ref.at[k // 2]
        product = dot(left[:, : 3 * rows], block_ref[k], 1, 0) + dot(
            left[:, 3 * rows :], diagonal[k], 1, 0
        )
        own_ref[k] = product[:share]
        send_ref[k] = bf(product[share:])


def mixer_backward(q, k, v, b, g, ids_row, first_row, inv, fresh, eff, state, maps, d_read, block, cols):
    heads, rows, values = v.shape
    units = block.shape[2]
    share = cols.shape[1] // 2
    bf16 = jnp.bfloat16
    return pl.pallas_call(
        mixer_backward_kernel,
        out_shape=(
            f32(*q.shape), f32(*k.shape), f32(*v.shape), f32(*b.shape), f32(*g.shape),
            f32(3, share, units), jax.ShapeDtypeStruct((3, share, units), bf16),
        ),
        scratch_shapes=[pltpu.VMEM((heads, DK, values), bf16)] * 4
        + [pltpu.VMEM((3, rows, units), bf16)]
        + [pltpu.SemaphoreType.DMA((2 * heads + 3,))] * 2,
        compiler_params=pltpu.CompilerParams(collective_id=2, has_side_effects=True),
        name="mixer_backward",
    )(q, k, v, b, g, ids_row, first_row, inv, fresh, eff, state, maps, d_read, block, cols)


def ffn_exchange_kernel(
    two_ref, down_ref, middle_ref, gate_ref, up_ref, hidden_ref, two_t_ref, top_t_ref,
    grad_out, block_out, g_out, x_out, red_send, red_in, sends, receives,
):
    rows = gate_ref.shape[0]
    share = x_out.shape[1] // 2
    s, t = lax.axis_index("seq"), lax.axis_index("tensor")
    low, high = s % 4, s // 4
    x_mate, z_mate = turned(s, 1), turned(s, 2)
    diagonal = turned(x_mate, 2)
    barrier = pltpu.get_barrier_semaphore()
    mates = [{"seq": x_mate}, {"seq": z_mate}, {"seq": diagonal}]
    mates += [{"tensor": turned(t, 1)}, {"tensor": turned(t, 2)}]
    for mate in mates:
        pl.semaphore_signal(barrier, inc=1, device_id=mate, device_id_type=pl.DeviceIdType.MESH)
    pl.semaphore_wait(barrier, len(mates))
    counter = [0]

    def push(src, dst, **where):
        at = counter[0]
        counter[0] += 1
        return send(src, dst, sends, receives, at, where)

    slot = [pl.ds(k * rows, rows) for k in range(4)]
    red_send[0] = bf(two_ref[...])
    red_send[1] = bf(down_ref[...])
    blocks = (gate_ref, up_ref, hidden_ref)
    others = [push(ref, g_out.at[k, slot[2], :], seq=z_mate) for k, ref in enumerate(blocks)]
    reds = [push(red_send.at[k], red_in.at[k], tensor=turned(t, 1)) for k in range(2)]
    others += [push(ref, g_out.at[k, slot[1], :], seq=x_mate) for k, ref in enumerate(blocks)]
    for k, ref in enumerate((two_t_ref, top_t_ref)):
        for at, mate in ((2, z_mate), (1, x_mate), (3, diagonal)):
            want = mate % 4
            for row, half in enumerate((high, 1 - high)):
                block = pl.ds(pl.multiple_of((half * 4 + want) * share, share), share)
                others.append(
                    push(
                        ref.at[block, :], x_out.at[k, pl.ds(row * share, share), slot[at]], seq=mate
                    )
                )
        for row, half in enumerate((high, 1 - high)):
            block = pl.ds(pl.multiple_of((half * 4 + low) * share, share), share)
            x_out[k, row * share : (row + 1) * share, :rows] = ref[block, :]
    for k, ref in enumerate(blocks):
        g_out[k, :rows, :] = ref[...]
    again = []
    for k in range(2):
        reds[k].wait()
        red_send[2 + k] = bf(wide(red_send[k]) + wide(red_in[k]))
        again.append(push(red_send.at[2 + k], red_in.at[2 + k], tensor=turned(t, 2)))
    again[0].wait()
    grad_out[...] = wide(red_send[2]) + wide(red_in[2])
    again[1].wait()
    block_out[...] = bf(middle_ref[...] + (wide(red_send[3]) + wide(red_in[3])))
    for copy in others:
        copy.wait()


def ffn_exchange(two_part, down_part, middle, gate, up, hidden, two_t, top_t):
    rows, model = middle.shape
    units = gate.shape[1]
    share = model // lax.axis_size("seq")
    bf16 = jnp.bfloat16
    return pl.pallas_call(
        ffn_exchange_kernel,
        out_shape=(
            f32(rows, model),
            jax.ShapeDtypeStruct((rows, model), bf16),
            jax.ShapeDtypeStruct((3, 3 * rows, units), bf16),
            jax.ShapeDtypeStruct((2, 2 * share, 4 * rows), bf16),
        ),
        in_specs=[pl.BlockSpec(memory_space=pltpu.VMEM)] * 8,
        out_specs=tuple([pl.BlockSpec(memory_space=pltpu.VMEM)] * 4),
        scratch_shapes=[pltpu.VMEM((4, rows, model), bf16)] * 2
        + [pltpu.SemaphoreType.DMA((32,))] * 2,
        compiler_params=pltpu.CompilerParams(collective_id=3, has_side_effects=True),
        name="ffn_exchange",
    )(two_part, down_part, middle, gate, up, hidden, two_t, top_t)


def tail_kernel(
    ge_ref, gate_ref, gated_ref, one_t_ref, mid_t_ref, w_ref, ab_ref, hidden_ref, gain_ref,
    middle_ref, rows_ref, pack_ref, out_gain_ref, ffn_own_ref, ffn_send_ref,
    in_out, out_out, grad_out, rows_out, norm_out, pack_out, gu_out, down_out,
    edge_in, late_f, gd_g, gt_g, lt_g, one_g, mid_g, part_own, part_send, part_in,
    red_send, red_in, rows_in, norm_send, norm_in, pack_in, pack_own, og_in, ffn_in,
    sends, receives,
):
    heads, ext, mixer = ge_ref.shape
    rows = gated_ref.shape[1]
    values = gated_ref.shape[2]
    edge = ext - rows
    seqs, tensors = lax.axis_size("seq"), lax.axis_size("tensor")
    s, t = lax.axis_index("seq"), lax.axis_index("tensor")
    share = in_out.shape[0]
    low, high = s % 4, s // 4
    counter = [0]

    def push(src, dst, **where):
        at = counter[0]
        counter[0] += 1
        return send(src, dst, sends, receives, at, where)

    greet((("seq", seqs), ("tensor", tensors)))
    x_mate, z_mate = turned(s, 1), turned(s, 2)
    slot = [pl.ds(k * rows, rows) for k in range(4)]

    edge_at = counter[0]
    counter[0] += 1
    edge_copy = pltpu.make_async_remote_copy(
        src_ref=ge_ref.at[:, pl.ds(0, 8), :],
        dst_ref=edge_in,
        send_sem=sends.at[edge_at],
        recv_sem=receives.at[edge_at],
        device_id={"seq": lax.rem(s + seqs - 1, seqs)},
        device_id_type=pl.DeviceIdType.MESH,
    )
    edge_copy.start()
    og = [
        push(out_gain_ref, og_in.at[t], tensor=lax.rem(t + k, tensors)) for k in range(1, tensors)
    ]
    og_in[t] = out_gain_ref[...]

    def gather_columns(src, dst):
        copies = []
        for k, bits in ((2, (2,)), (1, (1,)), (3, (1, 2))):
            mate, want = s, low
            for bit in bits:
                mate, want = turned(mate, bit), turned(want, bit)
            for row, half in enumerate((high, 1 - high)):
                block = pl.ds(pl.multiple_of((half * 4 + want) * share, share), share)
                copies.append(
                    push(src.at[block, :], dst.at[pl.ds(row * share, share), slot[k]], seq=mate)
                )
        for row, half in enumerate((high, 1 - high)):
            block = pl.ds(pl.multiple_of((half * 4 + low) * share, share), share)
            dst[row * share : (row + 1) * share, :rows] = src[block, :]
        return copies

    far = [push(gated_ref, gd_g.at[:, slot[2], :], seq=z_mate)]
    far.append(push(gate_ref, gt_g.at[:, slot[2], :], seq=z_mate))
    near = [push(gated_ref, gd_g.at[:, slot[1], :], seq=x_mate)]
    near.append(push(gate_ref, gt_g.at[:, slot[1], :], seq=x_mate))
    for h in range(heads):
        late_f[h] = ge_ref[h, edge:, :]
        gd_g[h, :rows, :] = gated_ref[h]
        gt_g[h, :rows, :] = gate_ref[h]
    ffn_copies = [
        push(ffn_send_ref.at[k], ffn_in.at[k], seq=turned(s, 4)) for k in range(3)
    ]
    edge_copy.wait()
    has_next = jnp.where(s == seqs - 1, 0.0, 1.0)
    for h in range(heads):
        late_f[h, rows - edge :, :] += edge_in[h, :edge, :] * has_next
        lt_g[h, :rows, :] = late_f[h].astype(jnp.bfloat16)
    part = ab_ref[...]
    columns = mixer + values
    for h in range(heads):
        at = h * columns + mixer
        part = part + dot(gate_ref[h], w_ref[:, at : at + values], 1, 1)
    late_far = push(lt_g.at[:, slot[0], :], lt_g.at[:, slot[2], :], seq=z_mate)
    late_near = push(lt_g.at[:, slot[0], :], lt_g.at[:, slot[1], :], seq=x_mate)
    mid_copies = gather_columns(mid_t_ref, mid_g)
    one_copies = gather_columns(one_t_ref, one_g)
    rows_copies = []
    for k in range(1, seqs):
        to = lax.rem(s + k, seqs)
        block = pl.ds(pl.multiple_of(to * share, share), share)
        rows_copies.append(push(rows_ref.at[:, block], rows_in.at[s], seq=to))
    rows_in[s] = rows_ref[:, pl.ds(pl.multiple_of(s * share, share), share)]
    for h in range(heads):
        at = h * columns
        part = part + dot(lt_g[h, :rows, :], w_ref[:, at : at + mixer], 1, 1)

    for step in range(tensors.bit_length() - 1):
        red_send[step] = part.astype(jnp.bfloat16)
        mate = turned(t, 1 << step)
        copy = push(red_send.at[step], red_in.at[step], tensor=mate)
        if step == 0:
            for c in og:
                c.wait()
            total = og_in[0]
            for k in range(1, tensors):
                total = total + og_in[k]
            pack_own[: total.shape[0], :] = total
            pack_own[total.shape[0] :, :] = pack_ref[...]
            for c in far:
                c.wait()
            far_on = [
                push(gd_g.at[:, slot[2], :], gd_g.at[:, slot[3], :], seq=x_mate),
                push(gt_g.at[:, slot[2], :], gt_g.at[:, slot[3], :], seq=x_mate),
            ]
        else:
            late_far.wait()
            late_on = push(lt_g.at[:, slot[2], :], lt_g.at[:, slot[3], :], seq=x_mate)
            pack_copies = [
                push(pack_own, pack_in.at[s], seq=lax.rem(s + k, seqs)) for k in range(1, seqs)
            ]
            pack_in[s] = pack_own[...]
        copy.wait()
        part = red_send[step].astype(jnp.float32) + red_in[step].astype(jnp.float32)

    stream = hidden_ref[...].astype(jnp.float32)
    gain = gain_ref[...]
    inv = lax.rsqrt(jnp.mean(stream * stream, axis=-1, keepdims=True) + EPSILON)
    scaled = part * gain
    grad_out[...] = (
        middle_ref[...] + inv * scaled
        - stream * (inv * inv * inv) * jnp.mean(scaled * stream, axis=-1, keepdims=True)
    )
    gain_part = (part * stream * inv).reshape(rows // 8, 8, stream.shape[1])
    norm_send[...] = jnp.sum(gain_part, axis=0)

    exchanged = []

    def halves(copies, sources, left, block, width, at):
        for c in copies:
            c.wait()
        for h in range(heads):
            product = dot(left[...], block[h], 1, 0)
            cols = slice(at + h * width, at + (h + 1) * width)
            part_own[:, cols] = product[:share]
            part_send[:, cols] = product[share:].astype(jnp.bfloat16)
        cols = pl.ds(at, heads * width)
        exchanged.append(push(part_send.at[:, cols], part_in.at[:, cols], seq=turned(s, 4)))

    halves(mid_copies + [near[0], far_on[0]], None, mid_g, gd_g, values, 0)
    halves(one_copies + [near[1], far_on[1]], None, one_g, gt_g, values, heads * values)
    norm_copies = []
    for k in range(1, seqs):
        to = lax.rem(s + k, seqs)
        block = pl.ds(pl.multiple_of(to * share, share), share)
        norm_copies.append(push(norm_send.at[:, block], norm_in.at[s], seq=to))
    norm_in[s] = norm_send[:, pl.ds(pl.multiple_of(s * share, share), share)]
    halves([late_near, late_on], None, one_g, lt_g, mixer, 2 * heads * values)

    for c in rows_copies:
        c.wait()
    for c in pack_copies:
        c.wait()
    for ref, out in ((rows_in, rows_out), (pack_in, pack_out)):
        total = ref[0]
        for k in range(1, seqs):
            total = total + ref[k]
        out[...] = total
    for c in norm_copies:
        c.wait()
    total = norm_in[0]
    for k in range(1, seqs):
        total = total + norm_in[k]
    norm_out[...] = jnp.sum(total, axis=0, keepdims=True)

    def finish(copy, at, width, out, first):
        copy.wait()
        for h in range(heads):
            cols = slice(at + h * width, at + (h + 1) * width)
            out[:, h, first : first + width] = part_own[:, cols] + part_in[:, cols].astype(
                jnp.float32
            )

    for k in range(3):
        ffn_copies[k].wait()
        summed = ffn_own_ref[k] + ffn_in[k].astype(jnp.float32)
        if k < 2:
            gu_out[:, k, :] = summed
        else:
            down_out[...] = summed
    finish(exchanged[0], 0, values, out_out, 0)
    finish(exchanged[1], heads * values, values, in_out, mixer)
    finish(exchanged[2], 2 * heads * values, mixer, in_out, 0)


def tail(
    ge, gate, gated, one_t, mid_t, w, ab, hidden, gain, middle, rows_small, pack, out_gain,
    ffn_own, ffn_send,
):
    heads, _, mixer = ge.shape
    _, rows, values = gated.shape
    model = hidden.shape[1]
    seqs, tensors = lax.axis_size("seq"), lax.axis_size("tensor")
    share = model // seqs
    wide_cols = heads * (mixer + 2 * values)
    joined_rows = pack.shape[0] + out_gain.shape[0]
    copies = 64
    bf16, f = jnp.bfloat16, jnp.float32
    return pl.pallas_call(
        tail_kernel,
        out_shape=(
            f32(share, heads, mixer + values),
            f32(share, heads, values),
            f32(rows, model),
            f32(rows_small.shape[0], share),
            f32(1, share),
            f32(joined_rows, pack.shape[1]),
            f32(share, 2, ffn_own.shape[2]),
            f32(share, ffn_own.shape[2]),
        ),
        in_specs=[pl.BlockSpec(memory_space=pltpu.VMEM)] * 15,
        out_specs=tuple([pl.BlockSpec(memory_space=pltpu.VMEM)] * 8),
        scratch_shapes=[
            pltpu.VMEM((heads, 8, mixer), f),
            pltpu.VMEM((heads, rows, mixer), f),
            pltpu.VMEM((heads, 4 * rows, values), bf16),
            pltpu.VMEM((heads, 4 * rows, values), bf16),
            pltpu.VMEM((heads, 4 * rows, mixer), bf16),
            pltpu.VMEM((2 * share, 4 * rows), bf16),
            pltpu.VMEM((2 * share, 4 * rows), bf16),
            pltpu.VMEM((share, wide_cols), f),
            pltpu.VMEM((share, wide_cols), bf16),
            pltpu.VMEM((share, wide_cols), bf16),
            pltpu.VMEM((2, rows, model), bf16),
            pltpu.VMEM((2, rows, model), bf16),
            pltpu.VMEM((seqs, rows_small.shape[0], share), f),
            pltpu.VMEM((8, model), f),
            pltpu.VMEM((seqs, 8, share), f),
            pltpu.VMEM((seqs, joined_rows, pack.shape[1]), f),
            pltpu.VMEM((joined_rows, pack.shape[1]), f),
            pltpu.VMEM((tensors, *out_gain.shape), f),
            pltpu.VMEM(ffn_send.shape, bf16),
            pltpu.SemaphoreType.DMA((copies,)),
            pltpu.SemaphoreType.DMA((copies,)),
        ],
        compiler_params=pltpu.CompilerParams(collective_id=0, has_side_effects=True),
        name="tail",
    )(
        ge, gate, gated, one_t, mid_t, w, ab, hidden, gain, middle, rows_small, pack, out_gain,
        ffn_own, ffn_send,
    )


def shards(
    hidden_in,
    seq_ids,
    norm_gain,
    w_in,
    w_ab,
    conv_w,
    a_log,
    dt_bias,
    out_gain,
    w_out,
    ffn_gain,
    w_gu,
    w_down,
    out_grad,
):
    row_count, model = hidden_in.shape
    heads = w_in.shape[1]
    width = conv_w.shape[1]
    mixer_width = conv_w.shape[2]
    count = lax.axis_size("seq")
    here = lax.axis_index("seq")
    first_row = here * row_count
    padded_ids = jnp.concatenate([jnp.full((width - 1,), -1, jnp.int32), seq_ids])
    ids_ext = lax.dynamic_slice_in_dim(padded_ids, first_row, row_count + width - 1)
    own_ids = ids_ext[width - 1 :]
    ids_row = own_ids.astype(jnp.float32)[None, :]
    same_first = (own_ids == ids_ext[width - 2]).astype(jnp.float32)[None, :]
    stream = hidden_in.astype(jnp.float32)
    normed_f, inv_one = rms_forward(stream, norm_gain)
    normed_one = normed_f.astype(jnp.bfloat16)
    projected = bf(
        jnp.einsum("td,dhp->htp", normed_one, w_in, preferred_element_type=jnp.float32)
    )
    mixer_ab = jnp.einsum("td,dhc->hct", normed_one, w_ab, preferred_element_type=jnp.float32)
    mixer_cols = projected[:, :, :mixer_width]
    edge_rows = passed_along(mixer_cols[:, row_count - width + 1 :], "seq", 1)
    extended = wide(jnp.concatenate([edge_rows, mixer_cols], axis=1))
    gate_in = wide(projected[:, :, mixer_width:])

    def prepare_local(ext_in, decay_in, rate_in, conv_in, alog_in, bias_in):
        return prepare(ext_in, decay_in, rate_in, conv_in, alog_in, bias_in, ids_ext)

    prepared, prepare_back = jax.vjp(
        prepare_local, extended, mixer_ab[:, 0], mixer_ab[:, 1], conv_w, a_log, dt_bias
    )
    share = model // count
    blocked = share % 128 == 0
    squared = blocked and count == 2 * 4 and lax.axis_size("tensor") == 4
    if squared:
        inverse, fresh, query_eff, reading, state_in, maps = mixer_forward(
            *prepared, ids_row, same_first
        )
    else:
        inverse, fresh, readings, carry = delta_forward(*prepared, ids_row, same_first)
        query_eff = readings[:, :, :DK]
        state_in, maps = state_before(carry)
        reading = readings[:, :, DK:] + bmm(query_eff, state_in)
    gated_f, gate_back = jax.vjp(output_gate, reading, gate_in, out_gain)
    gated = bf(gated_f)
    mixed_part = jnp.einsum("hte,dhe->td", gated, w_out, preferred_element_type=jnp.float32)
    mixed = exchanged_sum(mixed_part, "tensor", jnp.bfloat16)
    if not squared:
        mixed, maps = lax.optimization_barrier((mixed, maps))
    middle = stream + mixed
    normed_two_f, inv_two = rms_forward(middle, ffn_gain)
    normed_two = bf(normed_two_f)
    gate_part = jnp.dot(normed_two, w_gu[:, 0], preferred_element_type=jnp.float32)
    up_part = jnp.dot(normed_two, w_gu[:, 1], preferred_element_type=jnp.float32)
    hidden_ffn = bf(jax.nn.silu(gate_part) * up_part)
    ffn_part = jnp.einsum("tf,df->td", hidden_ffn, w_down, preferred_element_type=jnp.float32)
    grad_top = wide(out_grad)
    grad_hidden = jnp.dot(out_grad, w_down, preferred_element_type=jnp.float32)
    sigmoid_gate = jax.nn.sigmoid(gate_part)
    grad_gate_ffn = bf(
        grad_hidden * up_part * sigmoid_gate * (1.0 + gate_part * (1.0 - sigmoid_gate))
    )
    grad_up = bf(grad_hidden * gate_part * sigmoid_gate)
    normed_two_part = jnp.einsum(
        "tf,df->td", grad_gate_ffn, w_gu[:, 0], preferred_element_type=jnp.float32
    ) + jnp.einsum("tf,df->td", grad_up, w_gu[:, 1], preferred_element_type=jnp.float32)
    if squared:
        grad_normed_two, block_out, ffn_block, ffn_cols = ffn_exchange(
            normed_two_part, ffn_part, middle, grad_gate_ffn, grad_up, hidden_ffn,
            normed_two.T, out_grad.T,
        )
    else:
        ffn_width = w_down.shape[1]
        block_out = bf(middle + exchanged_sum(ffn_part, "tensor", jnp.bfloat16))
        grad_normed_two = exchanged_sum(normed_two_part, "tensor", jnp.bfloat16)
        ffn_grads = jnp.concatenate(
            [
                bf(jnp.einsum("td,tf->df", normed_two, grad_gate_ffn, preferred_element_type=jnp.float32)),
                bf(jnp.einsum("td,tf->df", normed_two, grad_up, preferred_element_type=jnp.float32)),
                bf(jnp.einsum("td,tf->df", out_grad, hidden_ffn, preferred_element_type=jnp.float32)),
            ],
            axis=1,
        )
        ffn_share = wide(lax.psum_scatter(ffn_grads, "seq", scatter_dimension=0, tiled=True))
        share_w_gu = ffn_share[:, : 2 * ffn_width].reshape(-1, 2, ffn_width)
        share_w_down = ffn_share[:, 2 * ffn_width :]
    grad_middle_norm, grad_ffn_gain = rms_backward(middle, inv_two, ffn_gain, grad_normed_two)
    grad_middle = grad_top + grad_middle_norm
    grad_middle_b = bf(grad_middle)
    grad_gated = jnp.einsum("td,dhe->hte", grad_middle_b, w_out, preferred_element_type=jnp.float32)
    grad_reading, grad_gate_in, gain_part = gate_back(grad_gated)
    if squared:
        *delta_grads, ffn_own, ffn_send = mixer_backward(
            *prepared, ids_row, same_first, inverse, fresh, query_eff, state_in, maps,
            grad_reading, ffn_block, ffn_cols,
        )
    else:
        carry_grad = jnp.einsum("htd,hte->hde", query_eff, grad_reading, precision=PRECISE)
        state_grad = grad_after(carry_grad, maps)
        delta_grads = delta_backward(
            *prepared, ids_row, same_first, inverse, fresh, state_in, grad_reading, state_grad
        )
    grad_extended, grad_decay, grad_rate, grad_conv_w, grad_a_log, grad_dt_bias = prepare_back(
        tuple(delta_grads)
    )
    grad_ab_b = bf(jnp.stack([grad_decay, grad_rate], axis=1))
    grad_w_ab = jnp.einsum(
        "td,hct->hcd", normed_one, grad_ab_b, preferred_element_type=jnp.float32
    )
    ab_part = jnp.einsum("hct,dhc->td", grad_ab_b, w_ab, preferred_element_type=jnp.float32)
    if squared:
        rows_small = jnp.concatenate(
            [grad_ffn_gain[None], grad_w_ab.reshape(2 * heads, model)], axis=0
        )
        rows_small = jnp.pad(rows_small, ((0, -rows_small.shape[0] % 8), (0, 0)))
        packed = jnp.concatenate([part.reshape(-1) for part in (grad_conv_w, grad_a_log, grad_dt_bias)])
        packed = jnp.pad(packed, (0, -packed.shape[0] % 1024)).reshape(-1, 128)
        gain_rows = jnp.pad(gain_part, (0, -gain_part.shape[0] % 1024)).reshape(-1, 128)
        share_w_in, share_w_out, grad_in, rows_sum, norm_gain_own, pack_sum, share_w_gu, share_w_down = tail(
            grad_extended, bf(grad_gate_in), gated, normed_one.T, grad_middle_b.T,
            w_in.reshape(model, -1), ab_part, hidden_in, norm_gain[None], grad_middle,
            rows_small, packed, gain_rows, ffn_own, ffn_send,
        )
        flat = pack_sum.reshape(-1)
        at = gain_rows.size
        conv_end = at + grad_conv_w.size
        return (
            block_out,
            grad_in,
            norm_gain_own[0],
            share_w_in,
            jnp.transpose(rows_sum[1 : 1 + 2 * heads].reshape(heads, 2, share), (2, 0, 1)),
            flat[at:conv_end].reshape(grad_conv_w.shape),
            flat[conv_end : conv_end + heads],
            flat[conv_end + heads : conv_end + 2 * heads],
            flat[: gain_part.shape[0]],
            share_w_out,
            rows_sum[0],
            share_w_gu,
            share_w_down,
        )
    returned_edge = passed_along(grad_extended[:, : width - 1], "seq", -1)
    grad_mixer = jnp.concatenate(
        [
            grad_extended[:, width - 1 : row_count],
            grad_extended[:, row_count:] + returned_edge,
        ],
        axis=1,
    )
    grad_projected = bf(jnp.concatenate([grad_mixer, grad_gate_in], axis=-1))
    w_out_grad = jnp.einsum(
        "td,hte->dhe", grad_middle_b, gated, preferred_element_type=jnp.float32
    )
    w_in_grad = jnp.einsum(
        "td,htp->dhp", normed_one, grad_projected, preferred_element_type=jnp.float32
    )
    mixer_grads = jnp.concatenate(
        [bf(w_in_grad).reshape(model, -1), bf(w_out_grad).reshape(model, -1)], axis=1
    )
    mixer_share = wide(lax.psum_scatter(mixer_grads, "seq", scatter_dimension=0, tiled=True))
    in_width = heads * w_in.shape[2]
    share_w_in = mixer_share[:, :in_width].reshape(-1, heads, w_in.shape[2])
    share_w_out = mixer_share[:, in_width:].reshape(-1, heads, w_out.shape[2])
    normed_one_part = jnp.einsum(
        "htp,dhp->td", grad_projected, w_in, preferred_element_type=jnp.float32
    )
    normed_one_part = normed_one_part + ab_part
    grad_normed_one = exchanged_sum(normed_one_part, "tensor", jnp.bfloat16)
    gain_total = exchanged_sum(gain_part, "tensor", jnp.float32)
    grad_norm_in, grad_norm_gain = rms_backward(stream, inv_one, norm_gain, grad_normed_one)
    grad_in = grad_middle + grad_norm_in
    parts = (
        grad_conv_w, gain_total, grad_ffn_gain, grad_norm_gain, grad_w_ab, grad_a_log, grad_dt_bias,
    )
    packed = jnp.concatenate([part.reshape(-1) for part in parts])
    length = packed.shape[0]
    packed = jnp.pad(packed, (0, -length % 1024)).reshape(-1, 128)
    total = exchanged_sum(packed, "seq", jnp.float32).reshape(-1)
    pieces, at = [], 0
    for part in parts:
        pieces.append(total[at : at + part.size].reshape(part.shape))
        at += part.size
    conv_sum, gain_sum, ffn_gain_sum, norm_gain_sum, w_ab_sum, a_log_sum, dt_bias_sum = pieces
    def own(whole, dim):
        return lax.dynamic_slice_in_dim(whole, here * share, share, dim)

    return (
        block_out,
        grad_in,
        own(norm_gain_sum, 0),
        share_w_in,
        jnp.transpose(own(w_ab_sum, 2), (2, 0, 1)),
        conv_sum,
        a_log_sum,
        dt_bias_sum,
        gain_sum,
        share_w_out,
        own(ffn_gain_sum, 0),
        share_w_gu,
        share_w_down,
    )


def solution(mesh):
    return jax.shard_map(
        shards,
        mesh=mesh,
        in_specs=(
            P("seq", None),
            P(),
            P(),
            P(None, "tensor", None),
            P(None, "tensor", None),
            P("tensor", None, None),
            P("tensor"),
            P("tensor"),
            P(),
            P(None, "tensor", None),
            P(),
            P(None, None, "tensor"),
            P(None, "tensor"),
            P("seq", None),
        ),
        out_specs=(
            P("seq", None),
            P("seq", None),
            P("seq"),
            P("seq", "tensor", None),
            P("seq", "tensor", None),
            P("tensor", None, None),
            P("tensor"),
            P("tensor"),
            P(),
            P("seq", "tensor", None),
            P("seq"),
            P("seq", None, "tensor"),
            P("seq", "tensor"),
        ),
        check_vma=False,
    )
```
